256 devices in a mesh: tm: 16 (over y, x), sx: 2 (over core), sy: 8 (over z).
Axes of the slice: x: 4, y: 4, z: 8, core: 2. Of those that a mesh axis runs over, the one named last changes fastest.
Arguments:
- frames: bfloat16 [32, 64, 128, 512], P('tm', 'sx', 'sy'), may hold values from -6 to 6
- input_weight: bfloat16 [3, 3, 512, 512], replicated, may hold values from -0.09375 to 0.09375
- output_weight: bfloat16 [3, 3, 512, 512], replicated, may hold values from -0.09375 to 0.09375
- pole_index: int32 [512], replicated, may hold values from 0 to 15
- gelu_scale: float32 [512], replicated, may hold values from 0.15 to 0.6
- start_state: float32 [64, 128, 512], P('sx', 'sy'), may hold values from -12 to 12
Outputs:
- result: bfloat16 [32, 64, 128, 512], P('tm', 'sx', 'sy')
The draws below stay inside these ranges and needn't reach their ends.
All inputs are finite; a program needn't handle non-finite values.
Results may differ from the reference program's by a relative error of at most 0.0049.
Values may be sent and summed in bfloat16 or wider, within the bound.
A program may use at most 128 MiB of HBM per device.

```python
import math
import jax
import jax.numpy as jnp
from jax import lax

C = 512
NPOLES = 16
TF = 32
H = 64
W = 128


def touch_ends(array, rng, least, high):
    longest = array.shape.index(max(array.shape))
    spots = []
    for shift in (0, 1):
        where = [jax.random.randint(jax.random.fold_in(rng, axis), (), 0, length) for axis, length in enumerate(array.shape)]
        where[longest] = (where[longest] + shift) % array.shape[longest]
        spots.append(tuple(where))
    return array.at[spots[0]].set(least).at[spots[1]].set(high)


def shard_levels(key, shape, cuts, low, largest):
    gain, own = 1.0, jax.random.fold_in(key, 6)
    for position, blocks in cuts:
        draws = jnp.exp(jax.random.uniform(jax.random.fold_in(own, position), (blocks,), jnp.float32, low / len(cuts), largest / len(cuts)))
        gain = gain * jnp.repeat(draws, shape[position] // blocks).reshape([-1 if axis == position else 1 for axis in range(len(shape))])
    return gain


def scatter_about(key, extent, deviation, limit, cuts=(), held_as=jnp.bfloat16):
    entries = jax.random.normal(key, extent, jnp.float32) * deviation
    if len(cuts) > 0:
        entries = shard_levels(key, extent, cuts, -0.22, 0.18) * entries
    return jnp.clip(entries, min=-limit, max=limit).astype(held_as)


def setup_inputs(seed: int = 0) -> dict:
    key_list = jax.random.split(jax.random.key(seed), 7)
    frames = scatter_about(key_list[0], (TF, H, W, C), 1.0, 6.0, ((0, 16), (1, 2), (2, 8)))
    input_weight = scatter_about(key_list[1], (3, 3, C, C), (9 * C) ** -0.5, 0.09375)
    output_weight = scatter_about(key_list[2], (3, 3, C, C), (9 * C) ** -0.5, 0.09375)
    pole_index = touch_ends(jax.random.randint(key_list[3], (C,), 0, NPOLES), jax.random.fold_in(key_list[3], 1), 0, NPOLES - 1).astype(jnp.int32)
    gelu_scale = jnp.clip(jnp.exp(jax.random.uniform(key_list[4], (C,), jnp.float32, math.log(0.15), math.log(0.6))), 0.15, 0.6)
    start_state = scatter_about(key_list[5], (H, W, C), 2.0, 12.0, ((0, 2), (1, 8)), jnp.float32)
    return {"frames": frames, "input_weight": input_weight, "output_weight": output_weight, "pole_index": pole_index, "gelu_scale": gelu_scale, "start_state": start_state}


def convolve(frame, weight):
    rows, cols, channels = frame.shape
    padded = jnp.pad(frame, ((1, 1), (1, 1), (0, 0)))
    total = jnp.zeros((rows * cols, channels), jnp.float32)
    for row_shift in range(3):
        for col_shift in range(3):
            window = padded[row_shift:row_shift + rows, col_shift:col_shift + cols, :].reshape(-1, channels)
            total = total + jnp.dot(window, weight[row_shift, col_shift], preferred_element_type=jnp.float32)
    return total.reshape(rows, cols, channels)


def reference(frames, input_weight, output_weight, pole_index, gelu_scale, start_state):
    decay = jnp.exp(-0.001 * jnp.exp(pole_index.astype(jnp.float32) * (math.log(300.0) / (NPOLES - 1))))

    def advance(state, frame):
        drive = convolve(frame, input_weight)
        state = decay * state + drive
        mixed = jax.nn.gelu(gelu_scale * state).astype(jnp.bfloat16)
        return state, convolve(mixed, output_weight).astype(jnp.bfloat16)

    final_state, outputs = lax.scan(advance, start_state, frames)
    return outputs
```

```python
import functools
import math

import jax
import jax.numpy as jnp
from jax import lax
from jax.experimental import pallas as pl
from jax.experimental.pallas import tpu as pltpu
from jax.sharding import PartitionSpec as P

NPOLES = 16
CHUNKS = 4
MESH = pl.DeviceIdType.MESH
F32 = jnp.float32
BF16 = jnp.bfloat16


def layer_kernel(
    sizes,
    frames_hbm, w1_hbm, w2_hbm, pole_ref, scale_ref, start_hbm, out_hbm,
    raw, wide, xf, xm, drive, w1, w2, ends, gathered, prefixes, carried, first, out,
    decay_ref, decay2_ref, edge_out, edge_in, side_out, side_in,
    frame_sem, w1_sem, w2_sem, first_sem, out_sem,
    col_send, col_recv, row_send, row_recv,
    end_send, end_recv, pre_send, pre_recv,
):
    peers, zs, rows, cols, ch = sizes
    n = CHUNKS
    step = rows // n
    split = peers // step
    lanes = ch // split
    me, sx, z = lax.axis_index("tm"), lax.axis_index("sx"), lax.axis_index("sy")
    other = 1 - sx
    right, left = lax.rem(z + 1, zs), lax.rem(z + zs - 1, zs)
    piece_row, piece_part = me // split, lax.rem(me, split)

    def row_of(lo, hi):
        return jnp.where(sx == 0, rows - hi, lo)

    def base(c):
        return row_of(c * step, (c + 1) * step)

    border = jnp.where(sx == 0, rows, 1)
    blank = jnp.where(sx == 0, 0, rows + 1)
    halo_there = jnp.where(sx == 0, 0, rows + 1)

    frame_copy = pltpu.make_async_copy(frames_hbm, raw, frame_sem)
    frame_copy.start()
    w1_copies = [pltpu.make_async_copy(w1_hbm.at[i], w1.at[i], w1_sem.at[i]) for i in range(3)]
    for copy in w1_copies:
        copy.start()

    barrier = pltpu.get_barrier_semaphore()
    for k in range(1, peers):
        pl.semaphore_signal(barrier, inc=1, device_id={"tm": lax.rem(me + k, peers)}, device_id_type=MESH)
    for where in ({"sy": left}, {"sy": right}, {"sx": other}):
        pl.semaphore_signal(barrier, inc=1, device_id=where, device_id_type=MESH)

    first_copies = []
    for c in range(n):
        copy = pltpu.make_async_copy(
            start_hbm.at[base(c) + piece_row, :, pl.ds(pl.multiple_of(piece_part * lanes, lanes), lanes)],
            first.at[c], first_sem.at[c],
        )
        copy.start()
        first_copies.append(copy)
    w2_copies = [pltpu.make_async_copy(w2_hbm.at[i], w2.at[i], w2_sem.at[i]) for i in range(3)]
    for copy in w2_copies:
        copy.start()

    decay = jnp.exp(-0.001 * jnp.exp(pole_ref[...].astype(F32) * (math.log(300.0) / (NPOLES - 1))))
    decay_ref[...] = decay
    for part in range(split):
        decay2_ref[part] = (decay * decay)[:, part * lanes : (part + 1) * lanes]
    for padded in (xf, xm):
        padded[:, pl.ds(blank, 1)] = jnp.zeros((2, 1, cols, 3 * ch), BF16)

    def side_refs(slot):
        return (edge_out, edge_in) if slot == n else (side_out.at[slot], side_in.at[slot])

    def side_copies(slot):
        src, dst = side_refs(slot)
        return [
            pltpu.make_async_remote_copy(
                src.at[d], dst.at[d], col_send.at[slot, d], col_recv.at[slot, d],
                device_id={"sy": to}, device_id_type=MESH,
            )
            for d, to in ((0, right), (1, left))
        ]

    def row_copy(padded, slot):
        return pltpu.make_async_remote_copy(
            padded.at[:, pl.ds(border, 1)], padded.at[:, pl.ds(halo_there, 1)],
            row_send.at[slot], row_recv.at[slot],
            device_id={"sx": other}, device_id_type=MESH,
        )

    def send_sides(slot, at, count):
        src = side_refs(slot)[0]
        for f in range(2):
            spot = pl.ds(f * rows + at, count)
            last, head = wide[spot, 7 + cols, :], wide[spot, 8, :]
            src[0, f] = last.astype(BF16)
            src[1, f] = head.astype(BF16)
        copies = side_copies(slot)
        for copy in copies:
            copy.start()
        return copies

    def place_sides(slot, at, count):
        dst = side_refs(slot)[1]
        for f in range(2):
            spot = pl.ds(f * rows + at, count)
            for d, col, kept in ((0, 7, z > 0), (1, 8 + cols, z < zs - 1)):
                wide[spot, col, :] = jnp.where(kept, dst[d, f].astype(F32), 0.0)

    def spread(padded, at, count):
        for f in range(2):
            for r in range(count):
                for j in range(3):
                    padded[f, at + r + 1, :, j * ch : (j + 1) * ch] = wide[f * rows + at + r, 7 + j : 7 + j + cols, :].astype(BF16)

    def conv(padded, weight, at, count):
        window = jnp.concatenate(
            [padded[:, pl.ds(at + i, count)].reshape(2 * count * cols, 3 * ch) for i in range(3)], axis=-1
        )
        return jnp.dot(window, weight[...].reshape(9 * ch, ch), preferred_element_type=F32).reshape(2, count, cols, ch)

    frame_copy.wait()

    def widen(r, _):
        for f in range(2):
            wide[f * rows + r, 8 : 8 + cols, :] = raw[f, r].astype(F32)
        return 0

    lax.fori_loop(0, rows, widen, 0, unroll=4)
    pl.semaphore_wait(barrier, peers + 2)
    waits = send_sides(n, 0, rows)
    for copy in waits:
        copy.wait_recv()
    place_sides(n, 0, rows)
    spread(xf, base(0), step)
    row_f = row_copy(xf, 0)
    row_f.start()
    sent = [copy.wait_send for copy in waits] + [row_f.wait_send]

    def rest(c, _):
        spread(xf, base(c), step)
        return 0

    lax.fori_loop(1, n, rest, 0)
    row_f.wait_recv()
    for copy in w1_copies:
        copy.wait()

    def all_of(ref, sem):
        return pltpu.make_async_copy(ref, ref, sem)

    def exchange(src, dst, send, recv, c):
        pltpu.make_async_copy(src.at[c, me], dst.at[c, me], recv.at[c]).start()
        for k in range(1, peers):
            to = lax.rem(me + k, peers)
            pltpu.make_async_remote_copy(
                src.at[c, to], dst.at[c, me], send.at[c], recv.at[c],
                device_id={"tm": to}, device_id_type=MESH,
            ).start()
        sent.append(all_of(src.at[c, pl.ds(0, peers - 1)], send.at[c]).wait)

    def drive_chunk(c):
        got = conv(xf, w1, base(c), step)
        drive[c] = got
        end = decay_ref[...].reshape(1, 1, ch) * got[0] + got[1]
        for r in range(step):
            for part in range(split):
                ends[c, r * split + part] = end[r, :, part * lanes : (part + 1) * lanes].astype(BF16)
        exchange(ends, gathered, end_send, end_recv, c)

    def prefix_chunk(c):
        first_copies[c].wait()
        all_of(gathered.at[c], end_recv.at[c]).wait()
        square = decay2_ref[pl.ds(piece_part, 1)].reshape(1, lanes)
        state = first[c]
        for i in range(peers):
            prefixes[c, i] = state.astype(BF16)
            if i < peers - 1:
                state = square * state + gathered[c, i].astype(F32)
        exchange(prefixes, carried, pre_send, pre_recv, c)

    def mix_chunk(c):
        all_of(carried.at[c], pre_recv.at[c]).wait()
        at = base(c)
        for r in range(step):
            state = jnp.concatenate([carried[c, r * split + part] for part in range(split)], axis=-1).astype(F32)
            for f in range(2):
                state = decay_ref[...] * state + drive[c, f, r]
                wide[f * rows + at + r, 8 : 8 + cols, :] = jax.nn.gelu(scale_ref[...] * state)
        return send_sides(c, at, step)

    row_m = row_copy(xm, 1)

    def lay_chunk(c, copies):
        at = base(c)
        for copy in copies:
            copy.wait_recv()
            sent.append(copy.wait_send)
        place_sides(c, at, step)
        spread(xm, at, step)
        if c == 0:
            row_m.start()
            sent.append(row_m.wait_send)

    def result_chunk(c):
        lo = max(c * step - 1, 0)
        hi = rows if c == n - 1 else (c + 1) * step - 1
        at = row_of(lo, hi)
        if c == 0:
            row_m.wait_recv()
            for copy in w2_copies:
                copy.wait()
        out[:, pl.ds(at, hi - lo)] = conv(xm, w2, at, hi - lo).astype(BF16)
        copy = pltpu.make_async_copy(out.at[:, pl.ds(at, hi - lo)], out_hbm.at[:, pl.ds(at, hi - lo)], out_sem.at[c])
        copy.start()
        sent.append(copy.wait)

    for c in range(n):
        drive_chunk(c)
        if c >= 2:
            prefix_chunk(c - 2)
    sides = {}
    for c in range(max(n - 2, 0), n):
        prefix_chunk(c)
    for c in range(n):
        sides[c] = mix_chunk(c)
        if c >= 1:
            lay_chunk(c - 1, sides[c - 1])
            result_chunk(c - 1)
    lay_chunk(n - 1, sides[n - 1])
    result_chunk(n - 1)
    for wait in sent:
        wait()


def on_device(peers, zs, frames, input_weight, output_weight, pole_index, gelu_scale, start_state):
    count, rows, cols, ch = frames.shape
    n = CHUNKS
    step = rows // n
    split = peers // step
    lanes = ch // split
    any_space = pl.BlockSpec(memory_space=pl.ANY)
    vmem = pl.BlockSpec(memory_space=pltpu.VMEM)
    dma = pltpu.SemaphoreType.DMA
    pieces = pltpu.VMEM((n, peers, cols, lanes), BF16)
    return pl.pallas_call(
        functools.partial(layer_kernel, (peers, zs, rows, cols, ch)),
        out_shape=jax.ShapeDtypeStruct(frames.shape, BF16),
        in_specs=[any_space, any_space, any_space, vmem, vmem, any_space],
        out_specs=any_space,
        scratch_shapes=[
            pltpu.VMEM((count, rows, cols, ch), BF16),
            pltpu.VMEM((count * rows, 32, ch), F32),
            pltpu.VMEM((count, rows + 2, cols, 3 * ch), BF16),
            pltpu.VMEM((count, rows + 2, cols, 3 * ch), BF16),
            pltpu.VMEM((n, count, step, cols, ch), F32),
            pltpu.VMEM((3, 3 * ch, ch), BF16),
            pltpu.VMEM((3, 3 * ch, ch), BF16),
            pieces, pieces, pieces, pieces,
            pltpu.VMEM((n, cols, lanes), F32),
            pltpu.VMEM((count, rows, cols, ch), BF16),
            pltpu.VMEM((1, ch), F32),
            pltpu.VMEM((split, 1, lanes), F32),
            pltpu.VMEM((2, count, rows, ch), BF16),
            pltpu.VMEM((2, count, rows, ch), BF16),
            pltpu.VMEM((n, 2, count, step, ch), BF16),
            pltpu.VMEM((n, 2, count, step, ch), BF16),
            dma, dma((3,)), dma((3,)), dma((n,)), dma((n,)),
            dma((n + 1, 2)), dma((n + 1, 2)), dma((2,)), dma((2,)),
            dma((n,)), dma((n,)), dma((n,)), dma((n,)),
        ],
        compiler_params=pltpu.CompilerParams(
            collective_id=0, has_side_effects=True, vmem_limit_bytes=56 << 20
        ),
        name="layer",
    )(
        frames,
        input_weight.reshape(3, 3 * ch, ch),
        output_weight.reshape(3, 3 * ch, ch),
        pole_index.reshape(1, ch),
        gelu_scale.reshape(1, ch),
        start_state,
    )


def solution(mesh):
    return jax.shard_map(
        functools.partial(on_device, mesh.shape["tm"], mesh.shape["sy"]),
        mesh=mesh,
        in_specs=(P("tm", "sx", "sy", None), P(), P(), P(), P(), P("sx", "sy", None)),
        out_specs=P("tm", "sx", "sy", None),
        check_vma=False,
    )
```

```python
import functools
import math

import jax
import jax.numpy as jnp
from jax import lax
from jax.experimental import pallas as pl
from jax.experimental.pallas import tpu as pltpu
from jax.sharding import PartitionSpec as P

NPOLES = 16
CHUNKS = 4
MESH = pl.DeviceIdType.MESH
F32 = jnp.float32
BF16 = jnp.bfloat16


def layer_kernel(
    sizes,
    frames_hbm, w1_hbm, w2_hbm, pole_hbm, scale_hbm, start_hbm, out,
    wide, xf, xm, drive, w1, w2, ends, gathered, prefixes, carried, first, pole_ref, scale_ref,
    decay_ref, decay2_ref, edge_out, edge_in, side_out, side_in,
    frame_sem, small_sem, w1_sem, w2_sem, first_sem, near_sem,
    col_send, col_recv, row_send, row_recv,
    end_send, end_recv, pre_send, pre_recv,
):
    peers, zs, rows, cols, ch = sizes
    side = math.isqrt(peers)
    n = CHUNKS
    step = rows // n
    split = peers // step
    lanes = ch // split
    me, sx, z = lax.axis_index("tm"), lax.axis_index("sx"), lax.axis_index("sy")
    other = 1 - sx
    right, left = lax.rem(z + 1, zs), lax.rem(z + zs - 1, zs)
    piece_row, piece_part = me // split, lax.rem(me, split)

    def row_of(lo, hi):
        return jnp.where(sx == 0, rows - hi, lo)

    def base(c):
        return row_of(c * step, (c + 1) * step)

    border = jnp.where(sx == 0, rows, 1)
    blank = jnp.where(sx == 0, 0, rows + 1)
    halo_there = jnp.where(sx == 0, 0, rows + 1)

    mid = pl.ds(ch, ch)
    frame_copy = pltpu.make_async_copy(frames_hbm, xf.at[:, pl.ds(1, rows), :, mid], frame_sem)
    frame_copy.start()

    def weight_copies(src, dst, sems):
        return [
            pltpu.make_async_copy(src.at[:, pl.ds(j * ch, ch)], dst.at[:, pl.ds(j * ch, ch)], sems.at[j])
            for j in range(3)
        ]

    small_copies = [
        pltpu.make_async_copy(pole_hbm, pole_ref, small_sem.at[0]),
        pltpu.make_async_copy(scale_hbm, scale_ref, small_sem.at[1]),
    ]
    for copy in small_copies:
        copy.start()
    w1_copies = weight_copies(w1_hbm, w1, w1_sem)
    for j in (1, 0, 2):
        w1_copies[j].start()

    y, x = me // side, lax.rem(me, side)
    around = [
        {"tm": y * side + lax.rem(x + 1, side)},
        {"tm": y * side + lax.rem(x + side - 1, side)},
        {"tm": lax.rem(y + 1, side) * side + x},
        {"tm": lax.rem(y + side - 1, side) * side + x},
    ]
    barrier = pltpu.get_barrier_semaphore()
    for where in [{"sy": left}, {"sy": right}, {"sx": other}] + around:
        pl.semaphore_signal(barrier, inc=1, device_id=where, device_id_type=MESH)

    def tell(k):
        for where in around:
            pl.semaphore_signal(near_sem.at[k], inc=1, device_id=where, device_id_type=MESH)

    def hear(k):
        pl.semaphore_wait(near_sem.at[k], len(around))

    first_copies = []
    for c in range(n):
        copy = pltpu.make_async_copy(
            start_hbm.at[base(c) + piece_row, :, pl.ds(pl.multiple_of(piece_part * lanes, lanes), lanes)],
            first.at[c], first_sem.at[c],
        )
        copy.start()
        first_copies.append(copy)
    w2_copies = weight_copies(w2_hbm, w2, w2_sem)
    for copy in w2_copies:
        copy.start()

    for padded in (xf, xm):
        padded[:, pl.ds(blank, 1)] = jnp.zeros((2, 1, cols, 3 * ch), BF16)

    def side_refs(slot):
        return (edge_out, edge_in) if slot == n else (side_out.at[slot], side_in.at[slot])

    def side_copies(slot):
        src, dst = side_refs(slot)
        return [
            pltpu.make_async_remote_copy(
                src.at[d], dst.at[d], col_send.at[slot, d], col_recv.at[slot, d],
                device_id={"sy": to}, device_id_type=MESH,
            )
            for d, to in ((0, right), (1, left))
        ]

    def row_copy(padded, slot):
        return pltpu.make_async_remote_copy(
            padded.at[:, pl.ds(border, 1)], padded.at[:, pl.ds(halo_there, 1)],
            row_send.at[slot], row_recv.at[slot],
            device_id={"sx": other}, device_id_type=MESH,
        )

    def send_sides(slot, at, count):
        src = side_refs(slot)[0]
        for f in range(2):
            spot = pl.ds(f * rows + at, count)
            last, head = wide[spot, 7 + cols, :], wide[spot, 8, :]
            src[0, f] = last.astype(BF16)
            src[1, f] = head.astype(BF16)
        if slot == n:
            pl.semaphore_wait(barrier, 3 + len(around))
            tell(0)
        copies = side_copies(slot)
        for copy in copies:
            copy.start()
        return copies

    def place_sides(slot, at, count):
        dst = side_refs(slot)[1]
        for f in range(2):
            spot = pl.ds(f * rows + at, count)
            for d, col, kept in ((0, 7, z > 0), (1, 8 + cols, z < zs - 1)):
                wide[spot, col, :] = jnp.where(kept, dst[d, f].astype(F32), 0.0)

    def spread(padded, at, count):
        for f in range(2):
            for r in range(count):
                for j in (0, 2):
                    padded[f, at + r + 1, :, j * ch : (j + 1) * ch] = wide[f * rows + at + r, 7 + j : 7 + j + cols, :].astype(BF16)

    def dots(padded, weight, at, count, js):
        left_side = jnp.concatenate(
            [
                padded[:, pl.ds(at + i, count), :, j * ch : (j + 1) * ch].reshape(2 * count * cols, ch)
                for i in range(3) for j in js
            ],
            axis=-1,
        )
        right_side = jnp.concatenate([weight[i, j * ch : (j + 1) * ch] for i in range(3) for j in js], axis=0)
        return jnp.dot(left_side, right_side, preferred_element_type=F32).reshape(2, count, cols, ch)

    frame_copy.wait()

    def widen(r, _):
        for f in range(2):
            wide[f * rows + r, 8 : 8 + cols, :] = xf[f, r + 1, :, ch : 2 * ch].astype(F32)
        return 0

    lax.fori_loop(0, rows, widen, 0, unroll=4)
    edges = send_sides(n, 0, rows)
    for copy in small_copies:
        copy.wait()
    decay = jnp.exp(-0.001 * jnp.exp(pole_ref[...].astype(F32) * (math.log(300.0) / (NPOLES - 1))))
    decay_ref[...] = decay
    for part in range(split):
        decay2_ref[part] = (decay * decay)[:, part * lanes : (part + 1) * lanes]
    w1_copies[1].wait()
    drive[1] = dots(xf, w1, base(1), step, (1,))
    hear(0)
    tell(1)
    for c in range(2, n - 1):
        drive[c] = dots(xf, w1, base(c), step, (1,))
    hear(1)
    tell(2)
    for copy in edges:
        copy.wait_recv()
    place_sides(n, 0, rows)
    spread(xf, base(0), step)
    row_f = row_copy(xf, 0)
    row_f.start()
    sent = [copy.wait_send for copy in edges] + [row_f.wait_send]

    def rest(c, _):
        spread(xf, base(c), step)
        return 0

    lax.fori_loop(1, n, rest, 0)
    w1_copies[0].wait()
    w1_copies[2].wait()

    def all_of(ref, sem):
        return pltpu.make_async_copy(ref, ref, sem)

    def exchange(src, dst, send, recv, c):
        pltpu.make_async_copy(src.at[c, me], dst.at[c, me], recv.at[c]).start()
        for k in range(1, peers):
            to = lax.rem(me + k, peers)
            pltpu.make_async_remote_copy(
                src.at[c, to], dst.at[c, me], send.at[c], recv.at[c],
                device_id={"tm": to}, device_id_type=MESH,
            ).start()
        sent.append(all_of(src.at[c, pl.ds(0, peers - 1)], send.at[c]).wait)

    def drive_chunk(c):
        if c == 0:
            row_f.wait_recv()
        if 1 <= c < n - 1:
            got = drive[c] + dots(xf, w1, base(c), step, (0, 2))
        else:
            got = dots(xf, w1, base(c), step, (0, 1, 2))
        drive[c] = got
        end = decay_ref[...].reshape(1, 1, ch) * got[0] + got[1]
        for r in range(step):
            for part in range(split):
                ends[c, r * split + part] = end[r, :, part * lanes : (part + 1) * lanes].astype(BF16)
        if c == 1:
            hear(2)
        exchange(ends, gathered, end_send, end_recv, c)

    def prefix_chunk(c):
        first_copies[c].wait()
        all_of(gathered.at[c], end_recv.at[c]).wait()
        square = decay2_ref[pl.ds(piece_part, 1)].reshape(1, lanes)
        state = first[c]
        for i in range(peers):
            prefixes[c, i] = state.astype(BF16)
            if i < peers - 1:
                state = square * state + gathered[c, i].astype(F32)
        exchange(prefixes, carried, pre_send, pre_recv, c)

    def mix_chunk(c):
        all_of(carried.at[c], pre_recv.at[c]).wait()
        at = base(c)
        for r in range(step):
            state = jnp.concatenate([carried[c, r * split + part] for part in range(split)], axis=-1).astype(F32)
            for f in range(2):
                state = decay_ref[...] * state + drive[c, f, r]
                mixed = jax.nn.gelu(scale_ref[...] * state)
                wide[f * rows + at + r, 8 : 8 + cols, :] = mixed
                xm[f, at + r + 1, :, ch : 2 * ch] = mixed.astype(BF16)
        sides[c] = send_sides(c, at, step)

    sides = {}
    row_m = row_copy(xm, 1)

    def lay_chunk(c):
        at = base(c)
        for copy in sides[c]:
            copy.wait_recv()
            sent.append(copy.wait_send)
        place_sides(c, at, step)
        spread(xm, at, step)
        if c == 0:
            row_m.start()
            sent.append(row_m.wait_send)

    def result_chunk(c):
        lo = max(c * step - 1, 0)
        hi = rows if c == n - 1 else (c + 1) * step - 1
        at = row_of(lo, hi)
        if c == n - 1:
            part = dots(xm, w2, at, hi - lo, (1,))
            lay_chunk(c)
            got = part + dots(xm, w2, at, hi - lo, (0, 2))
        else:
            got = dots(xm, w2, at, hi - lo, (0, 1, 2))
        out[:, pl.ds(at, hi - lo)] = got.astype(BF16)

    drive_chunk(1)
    drive_chunk(0)
    drive_chunk(2)
    prefix_chunk(1)
    drive_chunk(3)
    prefix_chunk(0)
    prefix_chunk(2)
    mix_chunk(1)
    prefix_chunk(3)
    mix_chunk(0)
    for copy in w2_copies:
        copy.wait()
    lay_chunk(1)
    lay_chunk(0)
    mix_chunk(2)
    result_chunk(1)
    row_m.wait_recv()
    result_chunk(0)
    lay_chunk(2)
    mix_chunk(3)
    result_chunk(2)
    result_chunk(3)
    for wait in sent:
        wait()


def on_device(peers, zs, frames, input_weight, output_weight, pole_index, gelu_scale, start_state):
    count, rows, cols, ch = frames.shape
    n = CHUNKS
    step = rows // n
    split = peers // step
    lanes = ch // split
    in_hbm = pl.BlockSpec(memory_space=pltpu.HBM)
    vmem = pl.BlockSpec(memory_space=pltpu.VMEM)
    dma = pltpu.SemaphoreType.DMA
    pieces = pltpu.VMEM((n, peers, cols, lanes), BF16)
    return pl.pallas_call(
        functools.partial(layer_kernel, (peers, zs, rows, cols, ch)),
        out_shape=jax.ShapeDtypeStruct(frames.shape, BF16),
        in_specs=[in_hbm] * 6,
        out_specs=vmem,
        scratch_shapes=[
            pltpu.VMEM((count * rows, 32, ch), F32),
            pltpu.VMEM((count, rows + 2, cols, 3 * ch), BF16),
            pltpu.VMEM((count, rows + 2, cols, 3 * ch), BF16),
            pltpu.VMEM((n, count, step, cols, ch), F32),
            pltpu.VMEM((3, 3 * ch, ch), BF16),
            pltpu.VMEM((3, 3 * ch, ch), BF16),
            pieces, pieces, pieces, pieces,
            pltpu.VMEM((n, cols, lanes), F32),
            pltpu.VMEM((1, ch), jnp.int32),
            pltpu.VMEM((1, ch), F32),
            pltpu.VMEM((1, ch), F32),
            pltpu.VMEM((split, 1, lanes), F32),
            pltpu.VMEM((2, count, rows, ch), BF16),
            pltpu.VMEM((2, count, rows, ch), BF16),
            pltpu.VMEM((n, 2, count, step, ch), BF16),
            pltpu.VMEM((n, 2, count, step, ch), BF16),
            dma, dma((2,)), dma((3,)), dma((3,)), dma((n,)), pltpu.SemaphoreType.REGULAR((3,)),
            dma((n + 1, 2)), dma((n + 1, 2)), dma((2,)), dma((2,)),
            dma((n,)), dma((n,)), dma((n,)), dma((n,)),
        ],
        compiler_params=pltpu.CompilerParams(
            collective_id=0, has_side_effects=True, vmem_limit_bytes=40 << 20
        ),
        name="layer",
    )(
        *(
            pltpu.with_memory_space_constraint(array, pltpu.HBM)
            for array in (
                frames,
                input_weight.reshape(3, 3 * ch, ch),
                output_weight.reshape(3, 3 * ch, ch),
                pole_index.reshape(1, ch),
                gelu_scale.reshape(1, ch),
                start_state,
            )
        )
    )


def solution(mesh):
    return jax.shard_map(
        functools.partial(on_device, mesh.shape["tm"], mesh.shape["sy"]),
        mesh=mesh,
        in_specs=(P("tm", "sx", "sy", None), P(), P(), P(), P(), P("sx", "sy", None)),
        out_specs=P("tm", "sx", "sy", None),
        check_vma=False,
    )
```

```python
import functools
import math

import jax
import jax.numpy as jnp
from jax import lax
from jax.experimental import pallas as pl
from jax.experimental.pallas import tpu as pltpu
from jax.sharding import PartitionSpec as P

NPOLES = 16
CHUNKS = 4
MESH = pl.DeviceIdType.MESH
F32 = jnp.float32
BF16 = jnp.bfloat16


def layer_kernel(
    sizes,
    frames_hbm, w1_hbm, w2_hbm, pole_hbm, scale_hbm, start_hbm, out,
    wide, xf, xm, drive, w1, w2, ends, gathered, prefixes, carried, first, pole_ref, scale_ref,
    decay_ref, decay2_ref, edge_out, edge_in, side_out, side_in, corner_out, corner_in, centers,
    frame_sem, small_sem, w1_sem, w2_sem, first_sem, near_sem,
    col_send, col_recv, row_send, row_recv, corner_send, corner_recv,
    end_send, end_recv, pre_send, pre_recv,
):
    peers, zs, rows, cols, ch = sizes
    side = math.isqrt(peers)
    n = CHUNKS
    step = rows // n
    split = peers // step
    lanes = ch // split
    me, sx, z = lax.axis_index("tm"), lax.axis_index("sx"), lax.axis_index("sy")
    other = 1 - sx
    right, left = lax.rem(z + 1, zs), lax.rem(z + zs - 1, zs)
    piece_row, piece_part = me // split, lax.rem(me, split)

    def row_of(lo, hi):
        return jnp.where(sx == 0, lo, rows - hi)

    def base(c):
        return row_of(c * step, (c + 1) * step)

    border = jnp.where(sx == 0, rows, 1)
    blank = jnp.where(sx == 0, 0, rows + 1)
    halo_there = blank
    halo_here = rows + 1 - blank

    mid = pl.ds(ch, ch)
    frame_copy = pltpu.make_async_copy(frames_hbm, xf.at[:, pl.ds(1, rows), :, mid], frame_sem)
    frame_copy.start()

    def weight_copies(src, dst, sems):
        return [
            pltpu.make_async_copy(src.at[:, pl.ds(j * ch, ch)], dst.at[:, pl.ds(j * ch, ch)], sems.at[j])
            for j in range(3)
        ]

    small_copies = [
        pltpu.make_async_copy(pole_hbm, pole_ref, small_sem.at[0]),
        pltpu.make_async_copy(scale_hbm, scale_ref, small_sem.at[1]),
    ]
    for copy in small_copies:
        copy.start()
    w1_copies = weight_copies(w1_hbm, w1, w1_sem)
    for j in (1, 0, 2):
        w1_copies[j].start()

    y, x = me // side, lax.rem(me, side)
    around = [
        {"tm": y * side + lax.rem(x + 1, side)},
        {"tm": y * side + lax.rem(x + side - 1, side)},
        {"tm": lax.rem(y + 1, side) * side + x},
        {"tm": lax.rem(y + side - 1, side) * side + x},
    ]
    diagonal = [{"sx": other, "sy": right}, {"sx": other, "sy": left}]
    barrier = pltpu.get_barrier_semaphore()
    for where in diagonal + [{"sy": left}, {"sy": right}, {"sx": other}] + around:
        pl.semaphore_signal(barrier, inc=1, device_id=where, device_id_type=MESH)

    def tell(k):
        for where in around:
            pl.semaphore_signal(near_sem.at[k], inc=1, device_id=where, device_id_type=MESH)

    def hear(k):
        pl.semaphore_wait(near_sem.at[k], len(around))

    first_copies = []
    for c in range(n):
        copy = pltpu.make_async_copy(
            start_hbm.at[base(c) + piece_row, :, pl.ds(pl.multiple_of(piece_part * lanes, lanes), lanes)],
            first.at[c], first_sem.at[c],
        )
        copy.start()
        first_copies.append(copy)
    w2_copies = weight_copies(w2_hbm, w2, w2_sem)
    for copy in w2_copies:
        copy.start()

    for padded in (xf, xm):
        padded[:, pl.ds(blank, 1)] = jnp.zeros((2, 1, cols, 3 * ch), BF16)

    def side_refs(slot):
        return (edge_out.at[slot - n], edge_in.at[slot - n]) if slot >= n else (side_out.at[slot], side_in.at[slot])

    def side_copies(slot):
        src, dst = side_refs(slot)
        return [
            pltpu.make_async_remote_copy(
                src.at[d], dst.at[d], col_send.at[slot, d], col_recv.at[slot, d],
                device_id={"sy": to}, device_id_type=MESH,
            )
            for d, to in ((0, right), (1, left))
        ]

    def row_copy(padded, slot):
        return pltpu.make_async_remote_copy(
            padded.at[:, pl.ds(border, 1), :, mid], padded.at[:, pl.ds(halo_there, 1), :, mid],
            row_send.at[slot], row_recv.at[slot],
            device_id={"sx": other}, device_id_type=MESH,
        )

    def border_copies(padded, slot):
        return [row_copy(padded, slot)] + [
            pltpu.make_async_remote_copy(
                corner_out.at[slot, d], corner_in.at[slot, d], corner_send.at[slot, d], corner_recv.at[slot, d],
                device_id=to, device_id_type=MESH,
            )
            for d, to in enumerate(diagonal)
        ]

    def fill_corners(slot):
        for d, col in ((0, 7 + cols), (1, 8)):
            corner_out[slot, d] = jnp.concatenate(
                [wide[f * rows + border - 1, col : col + 1, :] for f in range(2)], axis=0
            ).astype(BF16)

    def place_border(padded, slot, copies):
        for copy in copies:
            sent.append(copy.wait_send)
        for copy in copies[slot:]:
            copy.wait_recv()
        for f in range(2):
            at = 2 * rows + f
            wide[at, 8 : 8 + cols, :] = padded[f, halo_here, :, ch : 2 * ch].astype(F32)
            for d, col, kept in ((0, 7, z > 0), (1, 8 + cols, z < zs - 1)):
                wide[at, col : col + 1, :] = jnp.where(kept, corner_in[slot, d].astype(F32)[f : f + 1], 0.0)
            for j in (0, 2):
                padded[f, halo_here, :, j * ch : (j + 1) * ch] = wide[at, 7 + j : 7 + j + cols, :].astype(BF16)

    sent = []

    def send_sides(slot, at, count):
        src = side_refs(slot)[0]
        for f in range(2):
            spot = pl.ds(f * rows + at, count)
            last, head = wide[spot, 7 + cols, :], wide[spot, 8, :]
            src[0, f] = last.astype(BF16)
            src[1, f] = head.astype(BF16)
        if slot == n:
            fill_corners(0)
            pl.semaphore_wait(barrier, 5 + len(around))
            tell(0)
        copies = side_copies(slot)
        for copy in copies:
            copy.start()
        return copies

    def place_sides(slot, at, count):
        dst = side_refs(slot)[1]
        for f in range(2):
            spot = pl.ds(f * rows + at, count)
            for d, col, kept in ((0, 7, z > 0), (1, 8 + cols, z < zs - 1)):
                wide[spot, col, :] = jnp.where(kept, dst[d, f].astype(F32), 0.0)

    def spread(padded, at, count):
        for f in range(2):
            for r in range(count):
                for j in (0, 2):
                    padded[f, at + r + 1, :, j * ch : (j + 1) * ch] = wide[f * rows + at + r, 7 + j : 7 + j + cols, :].astype(BF16)

    def dots(padded, weight, at, count, js):
        left_side = jnp.concatenate(
            [
                padded[:, pl.ds(at + i, count), :, j * ch : (j + 1) * ch].reshape(2 * count * cols, ch)
                for i in range(3) for j in js
            ],
            axis=-1,
        )
        right_side = jnp.concatenate([weight[i, j * ch : (j + 1) * ch] for i in range(3) for j in js], axis=0)
        return jnp.dot(left_side, right_side, preferred_element_type=F32).reshape(2, count, cols, ch)

    frame_copy.wait()

    def widen(r, _):
        for f in range(2):
            wide[f * rows + r, 8 : 8 + cols, :] = xf[f, r + 1, :, ch : 2 * ch].astype(F32)
        return 0

    lax.fori_loop(0, rows, widen, 0, unroll=4)
    half = rows // 2
    early = send_sides(n, row_of(0, half), half)
    late = send_sides(n + 1, row_of(half, rows), half)
    border_f = border_copies(xf, 0)
    for copy in border_f:
        copy.start()
    for copy in small_copies:
        copy.wait()
    decay = jnp.exp(-0.001 * jnp.exp(pole_ref[...].astype(F32) * (math.log(300.0) / (NPOLES - 1))))
    decay_ref[...] = decay
    for part in range(split):
        decay2_ref[part] = (decay * decay)[:, part * lanes : (part + 1) * lanes]
    w1_copies[1].wait()
    for c in range(n - 1):
        drive[c] = dots(xf, w1, base(c), step, (1,))
        if c < 2:
            hear(c)
            tell(c + 1)
    for copy in early:
        copy.wait_recv()
        sent.append(copy.wait_send)
    place_sides(n, row_of(0, half), half)
    spread(xf, row_of(0, step + 1), step + 1)
    w1_copies[0].wait()
    w1_copies[2].wait()

    def all_of(ref, sem):
        return pltpu.make_async_copy(ref, ref, sem)

    def exchange(src, dst, send, recv, c):
        pltpu.make_async_copy(src.at[c, me], dst.at[c, me], recv.at[c]).start()
        for k in range(1, peers):
            to = lax.rem(me + k, peers)
            pltpu.make_async_remote_copy(
                src.at[c, to], dst.at[c, me], send.at[c], recv.at[c],
                device_id={"tm": to}, device_id_type=MESH,
            ).start()
        sent.append(all_of(src.at[c, pl.ds(0, peers - 1)], send.at[c]).wait)

    def drive_chunk(c):
        if c < n - 1:
            got = drive[c] + dots(xf, w1, base(c), step, (0, 2))
        else:
            got = dots(xf, w1, base(c), step, (0, 1, 2))
        drive[c] = got
        end = decay_ref[...].reshape(1, 1, ch) * got[0] + got[1]
        for r in range(step):
            for part in range(split):
                ends[c, r * split + part] = end[r, :, part * lanes : (part + 1) * lanes].astype(BF16)
        if c == 0:
            hear(2)
        exchange(ends, gathered, end_send, end_recv, c)

    def prefix_chunk(c):
        first_copies[c].wait()
        all_of(gathered.at[c], end_recv.at[c]).wait()
        square = decay2_ref[pl.ds(piece_part, 1)].reshape(1, lanes)
        state = first[c]
        for i in range(peers):
            prefixes[c, i] = state.astype(BF16)
            if i < peers - 1:
                state = square * state + gathered[c, i].astype(F32)
        exchange(prefixes, carried, pre_send, pre_recv, c)

    def mix_chunk(c):
        all_of(carried.at[c], pre_recv.at[c]).wait()
        at = base(c)
        for r in range(step):
            state = jnp.concatenate([carried[c, r * split + part] for part in range(split)], axis=-1).astype(F32)
            for f in range(2):
                state = decay_ref[...] * state + drive[c, f, r]
                mixed = jax.nn.gelu(scale_ref[...] * state)
                wide[f * rows + at + r, 8 : 8 + cols, :] = mixed
                xm[f, at + r + 1, :, ch : 2 * ch] = mixed.astype(BF16)
        if c == n - 1:
            fill_corners(1)
            for copy in border_m:
                copy.start()
        sides[c] = send_sides(c, at, step)

    sides = {}
    border_m = border_copies(xm, 1)

    def lay_chunk(c):
        at = base(c)
        for copy in sides[c]:
            copy.wait_recv()
            sent.append(copy.wait_send)
        place_sides(c, at, step)
        spread(xm, at, step)

    def window(c):
        lo = max(c * step - 1, 0)
        hi = rows if c == n - 1 else (c + 1) * step - 1
        return row_of(lo, hi), hi - lo

    def center_chunk(c):
        at, count = window(c)
        if c == n - 1:
            border_m[0].wait_recv()
        centers[c, :, pl.ds(0, count)] = dots(xm, w2, at, count, (1,))

    def result_chunk(c):
        at, count = window(c)
        got = centers[c, :, pl.ds(0, count)] + dots(xm, w2, at, count, (0, 2))
        out[:, pl.ds(at, count)] = got.astype(BF16)

    drive_chunk(0)
    for copy in late:
        copy.wait_recv()
        sent.append(copy.wait_send)
    place_sides(n + 1, row_of(half, rows), half)
    spread(xf, row_of(step + 1, 2 * step + 1), step)
    drive_chunk(1)
    spread(xf, row_of(2 * step + 1, rows), rows - 2 * step - 1)
    drive_chunk(2)
    place_border(xf, 0, border_f)
    drive_chunk(3)
    for c in range(n):
        prefix_chunk(c)
    for copy in w2_copies:
        copy.wait()
    mix_chunk(0)
    center_chunk(0)
    mix_chunk(1)
    center_chunk(1)
    mix_chunk(2)
    center_chunk(2)
    lay_chunk(0)
    result_chunk(0)
    mix_chunk(3)
    lay_chunk(1)
    result_chunk(1)
    lay_chunk(2)
    result_chunk(2)
    center_chunk(3)
    place_border(xm, 1, border_m)
    lay_chunk(3)
    result_chunk(3)
    for wait in sent:
        wait()


def on_device(peers, zs, frames, input_weight, output_weight, pole_index, gelu_scale, start_state):
    count, rows, cols, ch = frames.shape
    n = CHUNKS
    step = rows // n
    split = peers // step
    lanes = ch // split
    in_hbm = pl.BlockSpec(memory_space=pltpu.HBM)
    vmem = pl.BlockSpec(memory_space=pltpu.VMEM)
    dma = pltpu.SemaphoreType.DMA
    pieces = pltpu.VMEM((n, peers, cols, lanes), BF16)
    return pl.pallas_call(
        functools.partial(layer_kernel, (peers, zs, rows, cols, ch)),
        out_shape=jax.ShapeDtypeStruct(frames.shape, BF16),
        in_specs=[in_hbm] * 6,
        out_specs=vmem,
        scratch_shapes=[
            pltpu.VMEM((count * rows + count, 32, ch), F32),
            pltpu.VMEM((count, rows + 2, cols, 3 * ch), BF16),
            pltpu.VMEM((count, rows + 2, cols, 3 * ch), BF16),
            pltpu.VMEM((n, count, step, cols, ch), F32),
            pltpu.VMEM((3, 3 * ch, ch), BF16),
            pltpu.VMEM((3, 3 * ch, ch), BF16),
            pieces, pieces, pieces, pieces,
            pltpu.VMEM((n, cols, lanes), F32),
            pltpu.VMEM((1, ch), jnp.int32),
            pltpu.VMEM((1, ch), F32),
            pltpu.VMEM((1, ch), F32),
            pltpu.VMEM((split, 1, lanes), F32),
            pltpu.VMEM((2, 2, count, rows // 2, ch), BF16),
            pltpu.VMEM((2, 2, count, rows // 2, ch), BF16),
            pltpu.VMEM((n, 2, count, step, ch), BF16),
            pltpu.VMEM((n, 2, count, step, ch), BF16),
            pltpu.VMEM((2, 2, count, ch), BF16),
            pltpu.VMEM((2, 2, count, ch), BF16),
            pltpu.VMEM((n, count, step + 1, cols, ch), F32),
            dma, dma((2,)), dma((3,)), dma((3,)), dma((n,)), pltpu.SemaphoreType.REGULAR((3,)),
            dma((n + 2, 2)), dma((n + 2, 2)), dma((2,)), dma((2,)), dma((2, 2)), dma((2, 2)),
            dma((n,)), dma((n,)), dma((n,)), dma((n,)),
        ],
        compiler_params=pltpu.CompilerParams(
            collective_id=0, has_side_effects=True, vmem_limit_bytes=44 << 20
        ),
        name="layer",
    )(
        *(
            pltpu.with_memory_space_constraint(array, pltpu.HBM)
            for array in (
                frames,
                input_weight.reshape(3, 3 * ch, ch),
                output_weight.reshape(3, 3 * ch, ch),
                pole_index.reshape(1, ch),
                gelu_scale.reshape(1, ch),
                start_state,
            )
        )
    )


def solution(mesh):
    return jax.shard_map(
        functools.partial(on_device, mesh.shape["tm"], mesh.shape["sy"]),
        mesh=mesh,
        in_specs=(P("tm", "sx", "sy", None), P(), P(), P(), P(), P("sx", "sy", None)),
        out_specs=P("tm", "sx", "sy", None),
        check_vma=False,
    )
```

```python
import functools
import math

import jax
import jax.numpy as jnp
from jax import lax
from jax.experimental import pallas as pl
from jax.experimental.pallas import tpu as pltpu
from jax.sharding import PartitionSpec as P

NPOLES = 16
CHUNKS = 4
MESH = pl.DeviceIdType.MESH
F32 = jnp.float32
BF16 = jnp.bfloat16


def layer_kernel(
    sizes,
    frames_hbm, w1_hbm, w2_hbm, pole_hbm, scale_hbm, start_hbm, out,
    wide, xf, xm, drive, w1, w2, ends, gathered, prefixes, carried, first, pole_ref, scale_ref,
    decay_ref, decay2_ref, edge_out, edge_in, side_out, side_in, corner_out, corner_in, centers,
    frame_sem, small_sem, w1_sem, w2_sem, first_sem, near_sem,
    col_send, col_recv, row_send, row_recv, corner_send, corner_recv,
    end_send, end_recv, pre_send, pre_recv,
):
    peers, zs, rows, cols, ch = sizes
    side = math.isqrt(peers)
    n = CHUNKS
    step = rows // n
    split = peers // step
    lanes = ch // split
    me, sx, z = lax.axis_index("tm"), lax.axis_index("sx"), lax.axis_index("sy")
    other = 1 - sx
    right, left = lax.rem(z + 1, zs), lax.rem(z + zs - 1, zs)
    has_left, has_right = z > 0, z < zs - 1
    goes, comes = (has_right, has_left), (has_left, has_right)

    def only(condition, action):
        def run():
            pl.when(condition)(lambda: action() and None)
        return run

    piece_row, piece_part = me // split, lax.rem(me, split)

    def row_of(lo, hi):
        return jnp.where(sx == 0, lo, rows - hi)

    def base(c):
        return row_of(c * step, (c + 1) * step)

    border = jnp.where(sx == 0, rows, 1)
    blank = jnp.where(sx == 0, 0, rows + 1)
    halo_there = blank
    halo_here = rows + 1 - blank

    y, x = me // side, lax.rem(me, side)
    in_row = [{"tm": y * side + lax.rem(x + k, side)} for k in range(1, side)]
    in_column = [{"tm": lax.rem(y + k, side) * side + x} for k in range(1, side)]
    around = in_row + in_column
    diagonal = [{"sx": other, "sy": right}, {"sx": other, "sy": left}]
    barrier = pltpu.get_barrier_semaphore()
    for where in [{"sx": other}] + around:
        pl.semaphore_signal(barrier, inc=1, device_id=where, device_id_type=MESH)
    for condition, to, corner in ((has_right, right, diagonal[0]), (has_left, left, diagonal[1])):
        @pl.when(condition)
        def _(to=to, corner=corner):
            for where in ({"sy": to}, corner):
                pl.semaphore_signal(barrier, inc=1, device_id=where, device_id_type=MESH)
    expected = 1 + len(around) + 2 * jnp.where(has_left, 1, 0) + 2 * jnp.where(has_right, 1, 0)

    mid = pl.ds(ch, ch)
    quarter = rows // 4
    for f in range(2):
        for part in range(4):
            pltpu.make_async_copy(
                frames_hbm.at[f, pl.ds(part * quarter, quarter)],
                xf.at[f, pl.ds(1 + part * quarter, quarter), :, mid], frame_sem,
            ).start()

    class Weight:
        def __init__(self, src, dst, sem, j):
            self.copies = [
                pltpu.make_async_copy(src.at[i, pl.ds(j * ch, ch)], dst.at[i, pl.ds(j * ch, ch)], sem)
                for i in range(3)
            ]
            self.whole = pltpu.make_async_copy(src.at[:, pl.ds(j * ch, ch)], dst.at[:, pl.ds(j * ch, ch)], sem)

        def start(self):
            for copy in self.copies:
                copy.start()

        def wait(self):
            self.whole.wait()

    def weight_copies(src, dst, sems):
        return [Weight(src, dst, sems.at[j], j) for j in range(3)]

    small_copies = [
        pltpu.make_async_copy(pole_hbm, pole_ref, small_sem.at[0]),
        pltpu.make_async_copy(scale_hbm, scale_ref, small_sem.at[1]),
    ]
    for copy in small_copies:
        copy.start()
    w1_copies = weight_copies(w1_hbm, w1, w1_sem)
    w1_copies[1].start()

    def tell():
        for where in in_row:
            pl.semaphore_signal(near_sem, inc=1, device_id=where, device_id_type=MESH)

    def hear():
        pl.semaphore_wait(near_sem, len(in_row))

    first_copies = []
    for c in range(n):
        copy = pltpu.make_async_copy(
            start_hbm.at[base(c) + piece_row, :, pl.ds(pl.multiple_of(piece_part * lanes, lanes), lanes)],
            first.at[c], first_sem.at[c],
        )
        copy.start()
        first_copies.append(copy)
    w2_copies = weight_copies(w2_hbm, w2, w2_sem)

    for d in range(2):
        @pl.when(jnp.logical_not(comes[d]))
        def _(d=d):
            edge_in[:, d] = jnp.zeros_like(edge_in[:, d])
            side_in[:, d] = jnp.zeros_like(side_in[:, d])
            corner_in[:, d] = jnp.zeros_like(corner_in[:, d])
    for padded in (xf, xm):
        padded[:, pl.ds(blank, 1)] = jnp.zeros((2, 1, cols, 3 * ch), BF16)

    def side_refs(slot):
        return (edge_out.at[slot - n], edge_in.at[slot - n]) if slot >= n else (side_out.at[slot], side_in.at[slot])

    def side_copies(slot):
        src, dst = side_refs(slot)
        return [
            pltpu.make_async_remote_copy(
                src.at[d], dst.at[d], col_send.at[slot, d], col_recv.at[slot, d],
                device_id={"sy": to}, device_id_type=MESH,
            )
            for d, to in ((0, right), (1, left))
        ]

    def row_copy(padded, slot):
        return pltpu.make_async_remote_copy(
            padded.at[:, pl.ds(border, 1), :, mid], padded.at[:, pl.ds(halo_there, 1), :, mid],
            row_send.at[slot], row_recv.at[slot],
            device_id={"sx": other}, device_id_type=MESH,
        )

    def border_copies(padded, slot):
        return [row_copy(padded, slot)] + [
            pltpu.make_async_remote_copy(
                corner_out.at[slot, d], corner_in.at[slot, d], corner_send.at[slot, d], corner_recv.at[slot, d],
                device_id=to, device_id_type=MESH,
            )
            for d, to in enumerate(diagonal)
        ]

    def start_border(copies):
        copies[0].start()
        for d, copy in enumerate(copies[1:]):
            only(goes[d], copy.start)()

    def fill_corners(slot):
        for d, col in ((0, 7 + cols), (1, 8)):
            corner_out[slot, d] = jnp.concatenate(
                [wide[f * rows + border - 1, col : col + 1, :] for f in range(2)], axis=0
            ).astype(BF16)

    def place_border(padded, slot, copies):
        sent.append(copies[0].wait_send)
        if slot == 0:
            copies[0].wait_recv()
        take(copies[1:])
        for f in range(2):
            at = 2 * rows + f
            wide[at, 8 : 8 + cols, :] = padded[f, halo_here, :, ch : 2 * ch].astype(F32)
            for d, col in ((0, 7), (1, 8 + cols)):
                wide[at, col : col + 1, :] = corner_in[slot, d].astype(F32)[f : f + 1]
            for j in (0, 2):
                padded[f, halo_here, :, j * ch : (j + 1) * ch] = wide[at, 7 + j : 7 + j + cols, :].astype(BF16)

    sent = []

    def flush(kept=0):
        while len(sent) > kept:
            sent.pop(0)()

    def send_sides(slot, at, count):
        src = side_refs(slot)[0]
        for f in range(2):
            spot = pl.ds(f * rows + at, count)
            last, head = wide[spot, 7 + cols, :], wide[spot, 8, :]
            src[0, f] = last.astype(BF16)
            src[1, f] = head.astype(BF16)
        if slot == n:
            fill_corners(0)
            pl.semaphore_wait(barrier, expected)
            tell()
        copies = side_copies(slot)
        for d, copy in enumerate(copies):
            only(goes[d], copy.start)()
        return copies

    def take(copies):
        for d, copy in enumerate(copies):
            only(comes[d], copy.wait_recv)()
            sent.append(only(goes[d], copy.wait_send))

    def place_sides(slot, at, count):
        dst = side_refs(slot)[1]
        for f in range(2):
            spot = pl.ds(f * rows + at, count)
            for d, col in ((0, 7), (1, 8 + cols)):
                wide[spot, col, :] = dst[d, f].astype(F32)

    def spread(padded, at, count):
        for f in range(2):
            for r in range(count):
                for j in (0, 2):
                    padded[f, at + r + 1, :, j * ch : (j + 1) * ch] = wide[f * rows + at + r, 7 + j : 7 + j + cols, :].astype(BF16)

    def dots(padded, weight, at, count, js):
        left_side = jnp.concatenate(
            [
                padded[:, pl.ds(at + i, count), :, j * ch : (j + 1) * ch].reshape(2 * count * cols, ch)
                for i in range(3) for j in js
            ],
            axis=-1,
        )
        right_side = jnp.concatenate([weight[i, j * ch : (j + 1) * ch] for i in range(3) for j in js], axis=0)
        return jnp.dot(left_side, right_side, preferred_element_type=F32).reshape(2, count, cols, ch)

    pltpu.make_async_copy(frames_hbm, xf.at[:, pl.ds(1, rows), :, mid], frame_sem).wait()
    w1_copies[0].start()
    w1_copies[2].start()

    def widen(r, _):
        for f in range(2):
            wide[f * rows + r, 8 : 8 + cols, :] = xf[f, r + 1, :, ch : 2 * ch].astype(F32)
        return 0

    lax.fori_loop(0, rows, widen, 0, unroll=4)
    half = rows // 2
    early = send_sides(n, row_of(0, half), half)
    late = send_sides(n + 1, row_of(half, rows), half)
    border_f = border_copies(xf, 0)
    start_border(border_f)
    for copy in small_copies:
        copy.wait()
    decay = jnp.exp(-0.001 * jnp.exp(pole_ref[...].astype(F32) * (math.log(300.0) / (NPOLES - 1))))
    decay_ref[...] = decay
    for part in range(split):
        decay2_ref[part] = (decay * decay)[:, part * lanes : (part + 1) * lanes]
    w1_copies[1].wait()
    for c in range(n - 1):
        drive[c] = dots(xf, w1, base(c), step, (1,))
    take(early)
    for copy in w2_copies:
        copy.start()
    place_sides(n, row_of(0, half), half)
    spread(xf, row_of(0, step + 1), step + 1)
    w1_copies[0].wait()
    w1_copies[2].wait()

    def all_of(ref, sem):
        return pltpu.make_async_copy(ref, ref, sem)

    def exchange(src, dst, send, recv, c):
        pltpu.make_async_copy(src.at[c, me], dst.at[c, me], recv.at[c]).start()
        for k in range(1, peers):
            to = lax.rem(me + k, peers)
            pltpu.make_async_remote_copy(
                src.at[c, to], dst.at[c, me], send.at[c], recv.at[c],
                device_id={"tm": to}, device_id_type=MESH,
            ).start()
        sent.append(all_of(src.at[c, pl.ds(0, peers - 1)], send.at[c]).wait)

    def drive_chunk(c):
        if c < n - 1:
            got = drive[c] + dots(xf, w1, base(c), step, (0, 2))
        else:
            got = dots(xf, w1, base(c), step, (0, 1, 2))
        drive[c] = got
        end = decay_ref[...].reshape(1, 1, ch) * got[0] + got[1]
        for r in range(step):
            for part in range(split):
                ends[c, r * split + part] = end[r, :, part * lanes : (part + 1) * lanes].astype(BF16)
        if c == 0:
            hear()
        exchange(ends, gathered, end_send, end_recv, c)

    def prefix_chunk(c):
        first_copies[c].wait()
        all_of(gathered.at[c], end_recv.at[c]).wait()
        square = decay2_ref[pl.ds(piece_part, 1)].reshape(1, lanes)
        state = first[c]
        for i in range(peers):
            prefixes[c, i] = state.astype(BF16)
            if i < peers - 1:
                state = square * state + gathered[c, i].astype(F32)
        exchange(prefixes, carried, pre_send, pre_recv, c)

    def mix_chunk(c):
        if c == 0:
            flush(n)
        all_of(carried.at[c], pre_recv.at[c]).wait()
        at = base(c)
        for r in range(step):
            state = jnp.concatenate([carried[c, r * split + part] for part in range(split)], axis=-1).astype(F32)
            for f in range(2):
                state = decay_ref[...] * state + drive[c, f, r]
                mixed = jax.nn.gelu(scale_ref[...] * state)
                wide[f * rows + at + r, 8 : 8 + cols, :] = mixed
                xm[f, at + r + 1, :, ch : 2 * ch] = mixed.astype(BF16)
        if c == n - 1:
            fill_corners(1)
            start_border(border_m)
        sides[c] = send_sides(c, at, step)

    sides = {}
    border_m = border_copies(xm, 1)

    def lay_chunk(c):
        at = base(c)
        take(sides[c])
        place_sides(c, at, step)
        spread(xm, at, step)

    def window(c):
        lo = max(c * step - 1, 0)
        hi = rows if c == n - 1 else (c + 1) * step - 1
        return row_of(lo, hi), hi - lo

    def center_chunk(c):
        at, count = window(c)
        if c == n - 1:
            border_m[0].wait_recv()
        centers[c, :, pl.ds(0, count)] = dots(xm, w2, at, count, (1,))

    def result_chunk(c):
        at, count = window(c)
        got = centers[c, :, pl.ds(0, count)] + dots(xm, w2, at, count, (0, 2))
        out[:, pl.ds(at, count)] = got.astype(BF16)

    drive_chunk(0)
    take(late)
    place_sides(n + 1, row_of(half, rows), half)
    spread(xf, row_of(step + 1, 2 * step + 1), step)
    drive_chunk(1)
    spread(xf, row_of(2 * step + 1, rows), rows - 2 * step - 1)
    drive_chunk(2)
    place_border(xf, 0, border_f)
    drive_chunk(3)
    prefix_chunk(0)
    prefix_chunk(1)
    prefix_chunk(2)
    prefix_chunk(3)
    for copy in w2_copies:
        copy.wait()
    mix_chunk(0)
    center_chunk(0)
    mix_chunk(1)
    center_chunk(1)
    mix_chunk(2)
    center_chunk(2)
    mix_chunk(3)
    lay_chunk(0)
    result_chunk(0)
    lay_chunk(1)
    result_chunk(1)
    lay_chunk(2)
    result_chunk(2)
    center_chunk(3)
    place_border(xm, 1, border_m)
    lay_chunk(3)
    result_chunk(3)
    flush()


def on_device(peers, zs, frames, input_weight, output_weight, pole_index, gelu_scale, start_state):
    count, rows, cols, ch = frames.shape
    n = CHUNKS
    step = rows // n
    split = peers // step
    lanes = ch // split
    in_hbm = pl.BlockSpec(memory_space=pltpu.HBM)
    vmem = pl.BlockSpec(memory_space=pltpu.VMEM)
    dma = pltpu.SemaphoreType.DMA
    pieces = pltpu.VMEM((n, peers, cols, lanes), BF16)
    return pl.pallas_call(
        functools.partial(layer_kernel, (peers, zs, rows, cols, ch)),
        out_shape=jax.ShapeDtypeStruct(frames.shape, BF16),
        in_specs=[in_hbm] * 6,
        out_specs=vmem,
        scratch_shapes=[
            pltpu.VMEM((count * rows + count, 32, ch), F32),
            pltpu.VMEM((count, rows + 2, cols, 3 * ch), BF16),
            pltpu.VMEM((count, rows + 2, cols, 3 * ch), BF16),
            pltpu.VMEM((n, count, step, cols, ch), F32),
            pltpu.VMEM((3, 3 * ch, ch), BF16),
            pltpu.VMEM((3, 3 * ch, ch), BF16),
            pieces, pieces, pieces, pieces,
            pltpu.VMEM((n, cols, lanes), F32),
            pltpu.VMEM((1, ch), jnp.int32),
            pltpu.VMEM((1, ch), F32),
            pltpu.VMEM((1, ch), F32),
            pltpu.VMEM((split, 1, lanes), F32),
            pltpu.VMEM((2, 2, count, rows // 2, ch), BF16),
            pltpu.VMEM((2, 2, count, rows // 2, ch), BF16),
            pltpu.VMEM((n, 2, count, step, ch), BF16),
            pltpu.VMEM((n, 2, count, step, ch), BF16),
            pltpu.VMEM((2, 2, count, ch), BF16),
            pltpu.VMEM((2, 2, count, ch), BF16),
            pltpu.VMEM((n, count, step + 1, cols, ch), F32),
            dma, dma((2,)), dma((3,)), dma((3,)), dma((n,)), pltpu.SemaphoreType.REGULAR,
            dma((n + 2, 2)), dma((n + 2, 2)), dma((2,)), dma((2,)), dma((2, 2)), dma((2, 2)),
            dma((n,)), dma((n,)), dma((n,)), dma((n,)),
        ],
        compiler_params=pltpu.CompilerParams(
            collective_id=0, has_side_effects=True, vmem_limit_bytes=44 << 20
        ),
        name="layer",
    )(
        *(
            pltpu.with_memory_space_constraint(array, pltpu.HBM)
            for array in (
                frames,
                input_weight.reshape(3, 3 * ch, ch),
                output_weight.reshape(3, 3 * ch, ch),
                pole_index.reshape(1, ch),
                gelu_scale.reshape(1, ch),
                start_state,
            )
        )
    )


def solution(mesh):
    return jax.shard_map(
        functools.partial(on_device, mesh.shape["tm"], mesh.shape["sy"]),
        mesh=mesh,
        in_specs=(P("tm", "sx", "sy", None), P(), P(), P(), P(), P("sx", "sy", None)),
        out_specs=P("tm", "sx", "sy", None),
        check_vma=False,
    )
```

```python
import functools
import math

import jax
import jax.numpy as jnp
from jax import lax
from jax.experimental import pallas as pl
from jax.experimental.pallas import tpu as pltpu
from jax.sharding import PartitionSpec as P

NPOLES = 16
CHUNKS = 4
MESH = pl.DeviceIdType.MESH
F32 = jnp.float32
BF16 = jnp.bfloat16


def layer_kernel(
    sizes,
    frames_hbm, w1_hbm, w2_hbm, pole_hbm, scale_hbm, start_hbm, out,
    wide, xf, xm, drive, w1, w2, ends, gathered, prefixes, carried, first, pole_ref, scale_ref,
    decay_ref, decay2_ref, edge_out, edge_in, side_out, side_in, corner_out, corner_in, acc, beyond,
    frame_sem, small_sem, w1_sem, w2_sem, first_sem, near_sem,
    col_send, col_recv, row_send, row_recv, corner_send, corner_recv,
    end_send, end_recv, pre_send, pre_recv,
):
    peers, zs, rows, cols, ch = sizes
    side = math.isqrt(peers)
    n = CHUNKS
    step = rows // n
    split = peers // step
    lanes = ch // split
    me, sx, z = lax.axis_index("tm"), lax.axis_index("sx"), lax.axis_index("sy")
    other = 1 - sx
    right, left = lax.rem(z + 1, zs), lax.rem(z + zs - 1, zs)
    has_left, has_right = z > 0, z < zs - 1
    goes, comes = (has_right, has_left), (has_left, has_right)

    def only(condition, action):
        def run():
            pl.when(condition)(lambda: action() and None)
        return run

    piece_row, piece_part = me // split, lax.rem(me, split)

    def row_of(lo, hi):
        return jnp.where(sx == 0, lo, rows - hi)

    def base(c):
        return row_of(c * step, (c + 1) * step)

    border = jnp.where(sx == 0, rows, 1)
    blank = jnp.where(sx == 0, 0, rows + 1)
    halo_there = blank
    halo_here = rows + 1 - blank

    y, x = me // side, lax.rem(me, side)
    in_row = [{"tm": y * side + lax.rem(x + k, side)} for k in range(1, side)]
    in_column = [{"tm": lax.rem(y + k, side) * side + x} for k in range(1, side)]
    around = in_row + in_column
    diagonal = [{"sx": other, "sy": right}, {"sx": other, "sy": left}]
    barrier = pltpu.get_barrier_semaphore()
    for where in [{"sx": other}] + around:
        pl.semaphore_signal(barrier, inc=1, device_id=where, device_id_type=MESH)
    for condition, to, corner in ((has_right, right, diagonal[0]), (has_left, left, diagonal[1])):
        @pl.when(condition)
        def _(to=to, corner=corner):
            for where in ({"sy": to}, corner):
                pl.semaphore_signal(barrier, inc=1, device_id=where, device_id_type=MESH)
    expected = 1 + len(around) + 2 * jnp.where(has_left, 1, 0) + 2 * jnp.where(has_right, 1, 0)

    mid = pl.ds(ch, ch)
    quarter = rows // 4
    for f in range(2):
        for part in range(4):
            pltpu.make_async_copy(
                frames_hbm.at[f, pl.ds(part * quarter, quarter)],
                xf.at[f, pl.ds(1 + part * quarter, quarter), :, mid], frame_sem,
            ).start()

    class Weight:
        def __init__(self, src, dst, sem, j):
            self.copies = [
                pltpu.make_async_copy(src.at[i, pl.ds(j * ch, ch)], dst.at[i, pl.ds(j * ch, ch)], sem)
                for i in range(3)
            ]
            self.whole = pltpu.make_async_copy(src.at[:, pl.ds(j * ch, ch)], dst.at[:, pl.ds(j * ch, ch)], sem)

        def start(self):
            for copy in self.copies:
                copy.start()

        def wait(self):
            self.whole.wait()

    def weight_copies(src, dst, sems):
        return [Weight(src, dst, sems.at[j], j) for j in range(3)]

    small_copies = [
        pltpu.make_async_copy(pole_hbm, pole_ref, small_sem.at[0]),
        pltpu.make_async_copy(scale_hbm, scale_ref, small_sem.at[1]),
    ]
    for copy in small_copies:
        copy.start()
    w1_copies = weight_copies(w1_hbm, w1, w1_sem)
    w1_copies[1].start()

    def tell():
        for where in in_row:
            pl.semaphore_signal(near_sem, inc=1, device_id=where, device_id_type=MESH)

    def hear():
        pl.semaphore_wait(near_sem, len(in_row))

    first_copies = []
    for c in range(n):
        copy = pltpu.make_async_copy(
            start_hbm.at[base(c) + piece_row, :, pl.ds(pl.multiple_of(piece_part * lanes, lanes), lanes)],
            first.at[c], first_sem.at[c],
        )
        copy.start()
        first_copies.append(copy)
    w2_copies = weight_copies(w2_hbm, w2, w2_sem)

    for d in range(2):
        @pl.when(jnp.logical_not(comes[d]))
        def _(d=d):
            edge_in[:, d] = jnp.zeros_like(edge_in[:, d])
            side_in[:, d] = jnp.zeros_like(side_in[:, d])
            corner_in[:, d] = jnp.zeros_like(corner_in[:, d])
    for padded in (xf, xm):
        padded[:, pl.ds(blank, 1)] = jnp.zeros((2, 1, cols, 3 * ch), BF16)

    def side_refs(slot):
        return (edge_out.at[slot - n], edge_in.at[slot - n]) if slot >= n else (side_out.at[slot], side_in.at[slot])

    def side_copies(slot):
        src, dst = side_refs(slot)
        return [
            pltpu.make_async_remote_copy(
                src.at[d], dst.at[d], col_send.at[slot, d], col_recv.at[slot, d],
                device_id={"sy": to}, device_id_type=MESH,
            )
            for d, to in ((0, right), (1, left))
        ]

    def row_copy(padded, slot):
        return pltpu.make_async_remote_copy(
            padded.at[:, pl.ds(border, 1), :, mid], padded.at[:, pl.ds(halo_there, 1), :, mid],
            row_send.at[slot], row_recv.at[slot],
            device_id={"sx": other}, device_id_type=MESH,
        )

    def border_copies(padded, slot):
        return [row_copy(padded, slot)] + [
            pltpu.make_async_remote_copy(
                corner_out.at[slot, d], corner_in.at[slot, d], corner_send.at[slot, d], corner_recv.at[slot, d],
                device_id=to, device_id_type=MESH,
            )
            for d, to in enumerate(diagonal)
        ]

    def start_border(copies):
        copies[0].start()
        for d, copy in enumerate(copies[1:]):
            only(goes[d], copy.start)()

    def fill_corners(slot):
        for d, col in ((0, 7 + cols), (1, 8)):
            corner_out[slot, d] = jnp.concatenate(
                [wide[f * rows + border - 1, col : col + 1, :] for f in range(2)], axis=0
            ).astype(BF16)

    def place_border(padded, slot, copies):
        sent.append(copies[0].wait_send)
        if slot == 0:
            copies[0].wait_recv()
        take(copies[1:])
        for f in range(2):
            at = 2 * rows + f
            wide[at, 8 : 8 + cols, :] = padded[f, halo_here, :, ch : 2 * ch].astype(F32)
            for d, col in ((0, 7), (1, 8 + cols)):
                wide[at, col : col + 1, :] = corner_in[slot, d].astype(F32)[f : f + 1]
            for j in (0, 2):
                padded[f, halo_here, :, j * ch : (j + 1) * ch] = wide[at, 7 + j : 7 + j + cols, :].astype(BF16)

    sent = []

    def flush(kept=0):
        while len(sent) > kept:
            sent.pop(0)()

    def send_sides(slot, at, count):
        src = side_refs(slot)[0]
        for f in range(2):
            spot = pl.ds(f * rows + at, count)
            last, head = wide[spot, 7 + cols, :], wide[spot, 8, :]
            src[0, f] = last.astype(BF16)
            src[1, f] = head.astype(BF16)
        if slot == n:
            fill_corners(0)
            pl.semaphore_wait(barrier, expected)
            tell()
        copies = side_copies(slot)
        for d, copy in enumerate(copies):
            only(goes[d], copy.start)()
        return copies

    def take(copies):
        for d, copy in enumerate(copies):
            only(comes[d], copy.wait_recv)()
            sent.append(only(goes[d], copy.wait_send))

    def place_sides(slot, at, count):
        dst = side_refs(slot)[1]
        for f in range(2):
            spot = pl.ds(f * rows + at, count)
            for d, col in ((0, 7), (1, 8 + cols)):
                wide[spot, col, :] = dst[d, f].astype(F32)

    def spread(padded, at, count):
        for f in range(2):
            for r in range(count):
                for j in (0, 2):
                    padded[f, at + r + 1, :, j * ch : (j + 1) * ch] = wide[f * rows + at + r, 7 + j : 7 + j + cols, :].astype(BF16)

    def dots(padded, weight, at, count, js):
        left_side = jnp.concatenate(
            [
                padded[:, pl.ds(at + i, count), :, j * ch : (j + 1) * ch].reshape(2 * count * cols, ch)
                for i in range(3) for j in js
            ],
            axis=-1,
        )
        right_side = jnp.concatenate([weight[i, j * ch : (j + 1) * ch] for i in range(3) for j in js], axis=0)
        return jnp.dot(left_side, right_side, preferred_element_type=F32).reshape(2, count, cols, ch)

    pltpu.make_async_copy(frames_hbm, xf.at[:, pl.ds(1, rows), :, mid], frame_sem).wait()
    w1_copies[0].start()
    w1_copies[2].start()

    def widen(r, _):
        for f in range(2):
            wide[f * rows + r, 8 : 8 + cols, :] = xf[f, r + 1, :, ch : 2 * ch].astype(F32)
        return 0

    lax.fori_loop(0, rows, widen, 0, unroll=4)
    half = rows // 2
    early = send_sides(n, row_of(0, half), half)
    late = send_sides(n + 1, row_of(half, rows), half)
    border_f = border_copies(xf, 0)
    start_border(border_f)
    for copy in small_copies:
        copy.wait()
    decay = jnp.exp(-0.001 * jnp.exp(pole_ref[...].astype(F32) * (math.log(300.0) / (NPOLES - 1))))
    decay_ref[...] = decay
    for part in range(split):
        decay2_ref[part] = (decay * decay)[:, part * lanes : (part + 1) * lanes]
    w1_copies[1].wait()
    for c in range(n - 1):
        drive[c] = dots(xf, w1, base(c), step, (1,))
    take(early)
    for copy in w2_copies:
        copy.start()
    place_sides(n, row_of(0, half), half)
    spread(xf, row_of(0, step + 1), step + 1)
    w1_copies[0].wait()
    w1_copies[2].wait()

    def all_of(ref, sem):
        return pltpu.make_async_copy(ref, ref, sem)

    def exchange(src, dst, send, recv, c):
        pltpu.make_async_copy(src.at[c, me], dst.at[c, me], recv.at[c]).start()
        for k in range(1, peers):
            to = lax.rem(me + k, peers)
            pltpu.make_async_remote_copy(
                src.at[c, to], dst.at[c, me], send.at[c], recv.at[c],
                device_id={"tm": to}, device_id_type=MESH,
            ).start()
        sent.append(all_of(src.at[c, pl.ds(0, peers - 1)], send.at[c]).wait)

    def drive_chunk(c):
        if c < n - 1:
            got = drive[c] + dots(xf, w1, base(c), step, (0, 2))
        else:
            got = dots(xf, w1, base(c), step, (0, 1, 2))
        drive[c] = got
        end = decay_ref[...].reshape(1, 1, ch) * got[0] + got[1]
        for r in range(step):
            for part in range(split):
                ends[c, r * split + part] = end[r, :, part * lanes : (part + 1) * lanes].astype(BF16)
        if c == 0:
            hear()
        exchange(ends, gathered, end_send, end_recv, c)

    def prefix_chunk(c):
        first_copies[c].wait()
        all_of(gathered.at[c], end_recv.at[c]).wait()
        square = decay2_ref[pl.ds(piece_part, 1)].reshape(1, lanes)
        state = first[c]
        for i in range(peers):
            prefixes[c, i] = state.astype(BF16)
            if i < peers - 1:
                state = square * state + gathered[c, i].astype(F32)
        exchange(prefixes, carried, pre_send, pre_recv, c)

    def mix_chunk(c):
        if c == 0:
            flush(n)
        all_of(carried.at[c], pre_recv.at[c]).wait()
        at = base(c)
        for r in range(step):
            state = jnp.concatenate([carried[c, r * split + part] for part in range(split)], axis=-1).astype(F32)
            for f in range(2):
                state = decay_ref[...] * state + drive[c, f, r]
                mixed = jax.nn.gelu(scale_ref[...] * state)
                wide[f * rows + at + r, 8 : 8 + cols, :] = mixed
                xm[f, at + r + 1, :, ch : 2 * ch] = mixed.astype(BF16)
        if c == n - 1:
            fill_corners(1)
            start_border(border_m)
        sides[c] = send_sides(c, at, step)
        spread(xm, at, step)

    sides = {}
    border_m = border_copies(xm, 1)

    def window(c):
        lo = max(c * step - 1, 0)
        hi = rows if c == n - 1 else (c + 1) * step - 1
        return row_of(lo, hi), hi - lo

    def gather_chunk(c, js, more=False):
        at, count = window(c)
        got = dots(xm, w2, at, count, js)
        for f in range(2):
            spot = pl.ds(f * rows + at, count)
            acc[spot] = acc[spot] + got[f] if more else got[f]

    def border_row():
        border_m[0].wait_recv()
        sent.append(border_m[0].wait_send)
        for f in range(2):
            at = 2 * rows + f
            wide[at, 8 : 8 + cols, :] = xm[f, halo_here, :, ch : 2 * ch].astype(F32)
            for j in (0, 2):
                xm[f, halo_here, :, j * ch : (j + 1) * ch] = wide[at, 7 + j : 7 + j + cols, :].astype(BF16)

    def clear_sides():
        none = jnp.zeros((2 * rows + 2, ch), F32)
        for col in (7, 8 + cols):
            wide[:, col, :] = none

    def beyond_chunk(c):
        take(sides[c])
        at = pl.multiple_of(base(c) + 8, 8)
        for d in range(2):
            for f in range(2):
                beyond[d, f, pl.ds(at, step), :] = side_in[c, d, f].astype(F32)

    def beyond_corners():
        take(border_m[1:])
        for d in range(2):
            corner = corner_in[1, d].astype(F32)
            for f in range(2):
                row = corner[f : f + 1]
                beyond[d, f, 7:8, :] = jnp.where(sx == 1, row, 0.0)
                beyond[d, f, 8 + rows : 9 + rows, :] = jnp.where(sx == 0, row, 0.0)

    def finish():
        for d, j, col in ((0, 0, 0), (1, 2, cols - 1)):
            left_side = jnp.concatenate(
                [
                    jnp.concatenate([beyond[d, f, 7 + i : 7 + i + rows, :].astype(BF16) for i in range(3)], axis=-1)
                    for f in range(2)
                ],
                axis=0,
            )
            right_side = jnp.concatenate([w2[i, j * ch : (j + 1) * ch] for i in range(3)], axis=0)
            acc[:, col, :] = acc[:, col, :] + jnp.dot(left_side, right_side, preferred_element_type=F32)

        def narrow(r, _):
            for f in range(2):
                out[f, r] = acc[f * rows + r].astype(BF16)
            return 0

        lax.fori_loop(0, rows, narrow, 0, unroll=8)

    drive_chunk(0)
    take(late)
    place_sides(n + 1, row_of(half, rows), half)
    spread(xf, row_of(step + 1, 2 * step + 1), step)
    drive_chunk(1)
    spread(xf, row_of(2 * step + 1, rows), rows - 2 * step - 1)
    drive_chunk(2)
    place_border(xf, 0, border_f)
    drive_chunk(3)
    clear_sides()
    for c in range(n):
        prefix_chunk(c)
    for copy in w2_copies:
        copy.wait()
    every = (0, 1, 2)
    mix_chunk(0)
    gather_chunk(0, every)
    mix_chunk(1)
    gather_chunk(1, (1,))
    mix_chunk(2)
    gather_chunk(2, (1,))
    mix_chunk(3)
    gather_chunk(1, (0, 2), True)
    gather_chunk(2, (0, 2), True)
    border_row()
    gather_chunk(3, every)
    flush()
    for c in range(n):
        beyond_chunk(c)
    beyond_corners()
    finish()
    flush()


def on_device(peers, zs, frames, input_weight, output_weight, pole_index, gelu_scale, start_state):
    count, rows, cols, ch = frames.shape
    n = CHUNKS
    step = rows // n
    split = peers // step
    lanes = ch // split
    in_hbm = pl.BlockSpec(memory_space=pltpu.HBM)
    vmem = pl.BlockSpec(memory_space=pltpu.VMEM)
    dma = pltpu.SemaphoreType.DMA
    pieces = pltpu.VMEM((n, peers, cols, lanes), BF16)
    return pl.pallas_call(
        functools.partial(layer_kernel, (peers, zs, rows, cols, ch)),
        out_shape=jax.ShapeDtypeStruct(frames.shape, BF16),
        in_specs=[in_hbm] * 6,
        out_specs=vmem,
        scratch_shapes=[
            pltpu.VMEM((count * rows + count, 32, ch), F32),
            pltpu.VMEM((count, rows + 2, cols, 3 * ch), BF16),
            pltpu.VMEM((count, rows + 2, cols, 3 * ch), BF16),
            pltpu.VMEM((n, count, step, cols, ch), F32),
            pltpu.VMEM((3, 3 * ch, ch), BF16),
            pltpu.VMEM((3, 3 * ch, ch), BF16),
            pieces, pieces, pieces, pieces,
            pltpu.VMEM((n, cols, lanes), F32),
            pltpu.VMEM((1, ch), jnp.int32),
            pltpu.VMEM((1, ch), F32),
            pltpu.VMEM((1, ch), F32),
            pltpu.VMEM((split, 1, lanes), F32),
            pltpu.VMEM((2, 2, count, rows // 2, ch), BF16),
            pltpu.VMEM((2, 2, count, rows // 2, ch), BF16),
            pltpu.VMEM((n, 2, count, step, ch), BF16),
            pltpu.VMEM((n, 2, count, step, ch), BF16),
            pltpu.VMEM((2, 2, count, ch), BF16),
            pltpu.VMEM((2, 2, count, ch), BF16),
            pltpu.VMEM((count * rows, cols, ch), F32),
            pltpu.VMEM((2, count, rows + 16, ch), F32),
            dma, dma((2,)), dma((3,)), dma((3,)), dma((n,)), pltpu.SemaphoreType.REGULAR,
            dma((n + 2, 2)), dma((n + 2, 2)), dma((2,)), dma((2,)), dma((2, 2)), dma((2, 2)),
            dma((n,)), dma((n,)), dma((n,)), dma((n,)),
        ],
        compiler_params=pltpu.CompilerParams(
            collective_id=0, has_side_effects=True, vmem_limit_bytes=44 << 20
        ),
        name="layer",
    )(
        *(
            pltpu.with_memory_space_constraint(array, pltpu.HBM)
            for array in (
                frames,
                input_weight.reshape(3, 3 * ch, ch),
                output_weight.reshape(3, 3 * ch, ch),
                pole_index.reshape(1, ch),
                gelu_scale.reshape(1, ch),
                start_state,
            )
        )
    )


def solution(mesh):
    return jax.shard_map(
        functools.partial(on_device, mesh.shape["tm"], mesh.shape["sy"]),
        mesh=mesh,
        in_specs=(P("tm", "sx", "sy", None), P(), P(), P(), P(), P("sx", "sy", None)),
        out_specs=P("tm", "sx", "sy", None),
        check_vma=False,
    )
```

```python
import functools
import math

import jax
import jax.numpy as jnp
from jax import lax
from jax.experimental import pallas as pl
from jax.experimental.pallas import tpu as pltpu
from jax.sharding import PartitionSpec as P

NPOLES = 16
CHUNKS = 4
MESH = pl.DeviceIdType.MESH
F32 = jnp.float32
BF16 = jnp.bfloat16


def layer_kernel(
    sizes,
    frames_hbm, w1_hbm, w2_hbm, pole_hbm, scale_hbm, start_hbm, out,
    wide, xf, xm, drive, w1, w2, ends, gathered, prefixes, carried, first, pole_ref, scale_ref,
    decay_ref, decay2_ref, edge_out, edge_in, side_out, side_in, corner_out, corner_in, acc, beyond, tile,
    frame_sem, small_sem, w1_sem, w2_sem, first_sem, tile_sem, near_sem,
    col_send, col_recv, row_send, row_recv, corner_send, corner_recv,
    end_send, end_recv, pre_send, pre_recv,
):
    peers, zs, rows, cols, ch = sizes
    side = math.isqrt(peers)
    n = CHUNKS
    step = rows // n
    split = peers // step
    lanes = ch // split
    me, sx, z = lax.axis_index("tm"), lax.axis_index("sx"), lax.axis_index("sy")
    other = 1 - sx
    right, left = lax.rem(z + 1, zs), lax.rem(z + zs - 1, zs)
    has_left, has_right = z > 0, z < zs - 1
    goes, comes = (has_right, has_left), (has_left, has_right)

    def only(condition, action):
        def run():
            pl.when(condition)(lambda: action() and None)
        return run

    piece_row, piece_part = me // split, lax.rem(me, split)

    def row_of(lo, hi):
        return jnp.where(sx == 0, lo, rows - hi)

    def base(c):
        return row_of(c * step, (c + 1) * step)

    border = jnp.where(sx == 0, rows, 1)
    blank = jnp.where(sx == 0, 0, rows + 1)
    halo_there = blank
    halo_here = rows + 1 - blank

    y, x = me // side, lax.rem(me, side)
    in_row = [{"tm": y * side + lax.rem(x + k, side)} for k in range(1, side)]
    in_column = [{"tm": lax.rem(y + k, side) * side + x} for k in range(1, side)]
    around = in_row + in_column
    diagonal = [{"sx": other, "sy": right}, {"sx": other, "sy": left}]
    barrier = pltpu.get_barrier_semaphore()
    for where in [{"sx": other}] + around:
        pl.semaphore_signal(barrier, inc=1, device_id=where, device_id_type=MESH)
    for condition, to, corner in ((has_right, right, diagonal[0]), (has_left, left, diagonal[1])):
        @pl.when(condition)
        def _(to=to, corner=corner):
            for where in ({"sy": to}, corner):
                pl.semaphore_signal(barrier, inc=1, device_id=where, device_id_type=MESH)
    expected = 1 + len(around) + 2 * jnp.where(has_left, 1, 0) + 2 * jnp.where(has_right, 1, 0)

    mid = pl.ds(ch, ch)
    quarter = rows // 4
    for f in range(2):
        for part in range(4):
            pltpu.make_async_copy(
                frames_hbm.at[f, pl.ds(part * quarter, quarter)],
                xf.at[f, pl.ds(1 + part * quarter, quarter), :, mid], frame_sem,
            ).start()

    class Weight:
        def __init__(self, src, dst, sem, j):
            self.copies = [
                pltpu.make_async_copy(src.at[i, pl.ds(j * ch, ch)], dst.at[i, pl.ds(j * ch, ch)], sem)
                for i in range(3)
            ]
            self.whole = pltpu.make_async_copy(src.at[:, pl.ds(j * ch, ch)], dst.at[:, pl.ds(j * ch, ch)], sem)

        def start(self):
            for copy in self.copies:
                copy.start()

        def wait(self):
            self.whole.wait()

    def weight_copies(src, dst, sems):
        return [Weight(src, dst, sems.at[j], j) for j in range(3)]

    small_copies = [
        pltpu.make_async_copy(pole_hbm, pole_ref, small_sem.at[0]),
        pltpu.make_async_copy(scale_hbm, scale_ref, small_sem.at[1]),
    ]
    for copy in small_copies:
        copy.start()
    w1_copies = weight_copies(w1_hbm, w1, w1_sem)
    w1_copies[1].start()

    def tell():
        for where in in_row:
            pl.semaphore_signal(near_sem, inc=1, device_id=where, device_id_type=MESH)

    def hear():
        pl.semaphore_wait(near_sem, len(in_row))

    first_copies = []
    for c in range(n):
        copy = pltpu.make_async_copy(
            start_hbm.at[base(c) + piece_row, :, pl.ds(pl.multiple_of(piece_part * lanes, lanes), lanes)],
            first.at[c], first_sem.at[c],
        )
        copy.start()
        first_copies.append(copy)
    w2_copies = weight_copies(w2_hbm, w2, w2_sem)

    for d in range(2):
        @pl.when(jnp.logical_not(comes[d]))
        def _(d=d):
            edge_in[:, d] = jnp.zeros_like(edge_in[:, d])
            side_in[:, d] = jnp.zeros_like(side_in[:, d])
            corner_in[:, d] = jnp.zeros_like(corner_in[:, d])
    for padded in (xf, xm):
        padded[:, pl.ds(blank, 1)] = jnp.zeros((2, 1, cols, 3 * ch), BF16)

    def side_refs(slot):
        return (edge_out.at[slot - n], edge_in.at[slot - n]) if slot >= n else (side_out.at[slot], side_in.at[slot])

    def side_copies(slot):
        src, dst = side_refs(slot)
        return [
            pltpu.make_async_remote_copy(
                src.at[d], dst.at[d], col_send.at[slot, d], col_recv.at[slot, d],
                device_id={"sy": to}, device_id_type=MESH,
            )
            for d, to in ((0, right), (1, left))
        ]

    def row_copy(padded, slot):
        return pltpu.make_async_remote_copy(
            padded.at[:, pl.ds(border, 1), :, mid], padded.at[:, pl.ds(halo_there, 1), :, mid],
            row_send.at[slot], row_recv.at[slot],
            device_id={"sx": other}, device_id_type=MESH,
        )

    def border_copies(padded, slot):
        return [row_copy(padded, slot)] + [
            pltpu.make_async_remote_copy(
                corner_out.at[slot, d], corner_in.at[slot, d], corner_send.at[slot, d], corner_recv.at[slot, d],
                device_id=to, device_id_type=MESH,
            )
            for d, to in enumerate(diagonal)
        ]

    def start_border(copies):
        copies[0].start()
        for d, copy in enumerate(copies[1:]):
            only(goes[d], copy.start)()

    def fill_corners(slot):
        for d, col in ((0, 7 + cols), (1, 8)):
            corner_out[slot, d] = jnp.concatenate(
                [wide[f * rows + border - 1, col : col + 1, :] for f in range(2)], axis=0
            ).astype(BF16)

    def place_border(padded, slot, copies):
        sent.append(copies[0].wait_send)
        if slot == 0:
            copies[0].wait_recv()
        take(copies[1:])
        for f in range(2):
            at = 2 * rows + f
            wide[at, 8 : 8 + cols, :] = padded[f, halo_here, :, ch : 2 * ch].astype(F32)
            for d, col in ((0, 7), (1, 8 + cols)):
                wide[at, col : col + 1, :] = corner_in[slot, d].astype(F32)[f : f + 1]
            for j in (0, 2):
                padded[f, halo_here, :, j * ch : (j + 1) * ch] = wide[at, 7 + j : 7 + j + cols, :].astype(BF16)

    sent = []

    def flush(kept=0):
        while len(sent) > kept:
            sent.pop(0)()

    def send_sides(slot, at, count):
        src = side_refs(slot)[0]
        for f in range(2):
            spot = pl.ds(f * rows + at, count)
            last, head = wide[spot, 7 + cols, :], wide[spot, 8, :]
            src[0, f] = last.astype(BF16)
            src[1, f] = head.astype(BF16)
        if slot == n:
            fill_corners(0)
            pl.semaphore_wait(barrier, expected)
            tell()
        copies = side_copies(slot)
        for d, copy in enumerate(copies):
            only(goes[d], copy.start)()
        return copies

    def take(copies):
        for d, copy in enumerate(copies):
            only(comes[d], copy.wait_recv)()
            sent.append(only(goes[d], copy.wait_send))

    def place_sides(slot, at, count):
        dst = side_refs(slot)[1]
        for f in range(2):
            spot = pl.ds(f * rows + at, count)
            for d, col in ((0, 7), (1, 8 + cols)):
                wide[spot, col, :] = dst[d, f].astype(F32)

    def spread(padded, at, count):
        for f in range(2):
            for r in range(count):
                for j in (0, 2):
                    padded[f, at + r + 1, :, j * ch : (j + 1) * ch] = wide[f * rows + at + r, 7 + j : 7 + j + cols, :].astype(BF16)

    def dots(padded, weight, at, count, js):
        left_side = jnp.concatenate(
            [
                padded[:, pl.ds(at + i, count), :, j * ch : (j + 1) * ch].reshape(2 * count * cols, ch)
                for i in range(3) for j in js
            ],
            axis=-1,
        )
        right_side = jnp.concatenate([weight[i, j * ch : (j + 1) * ch] for i in range(3) for j in js], axis=0)
        return jnp.dot(left_side, right_side, preferred_element_type=F32).reshape(2, count, cols, ch)

    pltpu.make_async_copy(frames_hbm, xf.at[:, pl.ds(1, rows), :, mid], frame_sem).wait()
    w1_copies[0].start()
    w1_copies[2].start()

    def widen(r, _):
        for f in range(2):
            wide[f * rows + r, 8 : 8 + cols, :] = xf[f, r + 1, :, ch : 2 * ch].astype(F32)
        return 0

    lax.fori_loop(0, rows, widen, 0, unroll=4)
    half = rows // 2
    early = send_sides(n, row_of(0, half), half)
    late = send_sides(n + 1, row_of(half, rows), half)
    border_f = border_copies(xf, 0)
    start_border(border_f)
    for copy in small_copies:
        copy.wait()
    decay = jnp.exp(-0.001 * jnp.exp(pole_ref[...].astype(F32) * (math.log(300.0) / (NPOLES - 1))))
    decay_ref[...] = decay
    for part in range(split):
        decay2_ref[part] = (decay * decay)[:, part * lanes : (part + 1) * lanes]
    w1_copies[1].wait()
    for c in range(n - 1):
        drive[c] = dots(xf, w1, base(c), step, (1,))
    take(early)
    for copy in w2_copies:
        copy.start()
    tile_copy = pltpu.make_async_copy(start_hbm, tile, tile_sem)
    only(me == 0, tile_copy.start)()
    place_sides(n, row_of(0, half), half)
    spread(xf, row_of(0, step + 1), step + 1)
    w1_copies[0].wait()
    w1_copies[2].wait()

    def all_of(ref, sem):
        return pltpu.make_async_copy(ref, ref, sem)

    def transfer(src, dst, send, recv, c, to):
        return pltpu.make_async_remote_copy(
            src.at[c, to], dst.at[c, me], send.at[c], recv.at[c], device_id={"tm": to}, device_id_type=MESH
        )

    is_last, is_first = me == peers - 1, me == 0

    def send_ends(c):
        @pl.when(jnp.logical_not(is_last))
        def _():
            pltpu.make_async_copy(ends.at[c, me], gathered.at[c, me], end_recv.at[c]).start()
            for k in range(1, peers):
                transfer(ends, gathered, end_send, end_recv, c, lax.rem(me + k, peers)).start()

        sent.append(only(jnp.logical_not(is_last), all_of(ends.at[c, pl.ds(0, peers - 1)], end_send.at[c]).wait))

    def send_prefixes(c):
        @pl.when(jnp.logical_not(is_first))
        def _():
            pltpu.make_async_copy(prefixes.at[c, me], carried.at[c, me], pre_recv.at[c]).start()

        for k in range(1, peers):
            to = lax.rem(me + k, peers)
            only(to != 0, transfer(prefixes, carried, pre_send, pre_recv, c, to).start)()

        def settle():
            only(is_first, all_of(prefixes.at[c, pl.ds(0, peers - 1)], pre_send.at[c]).wait)()
            only(jnp.logical_not(is_first), all_of(prefixes.at[c, pl.ds(0, peers - 2)], pre_send.at[c]).wait)()

        sent.append(settle)

    def drive_chunk(c):
        if c < n - 1:
            got = drive[c] + dots(xf, w1, base(c), step, (0, 2))
        else:
            got = dots(xf, w1, base(c), step, (0, 1, 2))
        drive[c] = got
        end = decay_ref[...].reshape(1, 1, ch) * got[0] + got[1]
        for r in range(step):
            for part in range(split):
                ends[c, r * split + part] = end[r, :, part * lanes : (part + 1) * lanes].astype(BF16)
        if c == 0:
            hear()
        send_ends(c)

    def prefix_chunk(c):
        first_copies[c].wait()
        all_of(gathered.at[c, pl.ds(0, peers - 1)], end_recv.at[c]).wait()
        square = decay2_ref[pl.ds(piece_part, 1)].reshape(1, lanes)
        state = first[c]
        for i in range(peers):
            prefixes[c, i] = state.astype(BF16)
            if i < peers - 1:
                state = square * state + gathered[c, i].astype(F32)
        send_prefixes(c)

    def mix_chunk(c):
        if c == 0:
            flush(n)
        only(jnp.logical_not(is_first), all_of(carried.at[c], pre_recv.at[c]).wait)()
        at = base(c)
        for r in range(step):
            state = jnp.concatenate([carried[c, r * split + part] for part in range(split)], axis=-1).astype(F32)
            for f in range(2):
                state = decay_ref[...] * state + drive[c, f, r]
                mixed = jax.nn.gelu(scale_ref[...] * state)
                wide[f * rows + at + r, 8 : 8 + cols, :] = mixed
                xm[f, at + r + 1, :, ch : 2 * ch] = mixed.astype(BF16)
        if c == n - 1:
            fill_corners(1)
            start_border(border_m)
        sides[c] = send_sides(c, at, step)
        spread(xm, at, step)

    sides = {}
    border_m = border_copies(xm, 1)

    def window(c):
        lo = max(c * step - 1, 0)
        hi = rows if c == n - 1 else (c + 1) * step - 1
        return row_of(lo, hi), hi - lo

    def gather_chunk(c, js, more=False):
        at, count = window(c)
        got = dots(xm, w2, at, count, js)
        for f in range(2):
            spot = pl.ds(f * rows + at, count)
            acc[spot] = acc[spot] + got[f] if more else got[f]

    def border_row():
        border_m[0].wait_recv()
        sent.append(border_m[0].wait_send)
        for f in range(2):
            at = 2 * rows + f
            wide[at, 8 : 8 + cols, :] = xm[f, halo_here, :, ch : 2 * ch].astype(F32)
            for j in (0, 2):
                xm[f, halo_here, :, j * ch : (j + 1) * ch] = wide[at, 7 + j : 7 + j + cols, :].astype(BF16)

    def clear_sides():
        none = jnp.zeros((2 * rows + 2, ch), F32)
        for col in (7, 8 + cols):
            wide[:, col, :] = none

    def beyond_chunk(c):
        take(sides[c])
        at = pl.multiple_of(base(c) + 8, 8)
        for d in range(2):
            for f in range(2):
                beyond[d, f, pl.ds(at, step), :] = side_in[c, d, f].astype(F32)

    def beyond_corners():
        take(border_m[1:])
        for d in range(2):
            corner = corner_in[1, d].astype(F32)
            for f in range(2):
                row = corner[f : f + 1]
                beyond[d, f, 7:8, :] = jnp.where(sx == 1, row, 0.0)
                beyond[d, f, 8 + rows : 9 + rows, :] = jnp.where(sx == 0, row, 0.0)

    def finish():
        for d, j, col in ((0, 0, 0), (1, 2, cols - 1)):
            left_side = jnp.concatenate(
                [
                    jnp.concatenate([beyond[d, f, 7 + i : 7 + i + rows, :].astype(BF16) for i in range(3)], axis=-1)
                    for f in range(2)
                ],
                axis=0,
            )
            right_side = jnp.concatenate([w2[i, j * ch : (j + 1) * ch] for i in range(3)], axis=0)
            acc[:, col, :] = acc[:, col, :] + jnp.dot(left_side, right_side, preferred_element_type=F32)

        def narrow(r, _):
            for f in range(2):
                out[f, r] = acc[f * rows + r].astype(BF16)
            return 0

        lax.fori_loop(0, rows, narrow, 0, unroll=8)

    drive_chunk(0)
    take(late)
    place_sides(n + 1, row_of(half, rows), half)
    spread(xf, row_of(step + 1, 2 * step + 1), step)
    drive_chunk(1)
    spread(xf, row_of(2 * step + 1, rows), rows - 2 * step - 1)
    drive_chunk(2)
    place_border(xf, 0, border_f)
    drive_chunk(3)
    clear_sides()

    @pl.when(is_first)
    def _():
        tile_copy.wait()
        for c in range(n):
            for r in range(step):
                for part in range(split):
                    carried[c, r * split + part] = tile[
                        base(c) + r, :, part * lanes : (part + 1) * lanes
                    ].astype(BF16)

    for c in range(n):
        prefix_chunk(c)
    for copy in w2_copies:
        copy.wait()
    every = (0, 1, 2)
    mix_chunk(0)
    gather_chunk(0, every)
    mix_chunk(1)
    gather_chunk(1, (1,))
    mix_chunk(2)
    gather_chunk(2, (1,))
    mix_chunk(3)
    gather_chunk(1, (0, 2), True)
    gather_chunk(2, (0, 2), True)
    border_row()
    gather_chunk(3, every)
    flush()
    for c in range(n):
        beyond_chunk(c)
    beyond_corners()
    finish()
    flush()


def on_device(peers, zs, frames, input_weight, output_weight, pole_index, gelu_scale, start_state):
    count, rows, cols, ch = frames.shape
    n = CHUNKS
    step = rows // n
    split = peers // step
    lanes = ch // split
    in_hbm = pl.BlockSpec(memory_space=pltpu.HBM)
    vmem = pl.BlockSpec(memory_space=pltpu.VMEM)
    dma = pltpu.SemaphoreType.DMA
    pieces = pltpu.VMEM((n, peers, cols, lanes), BF16)
    return pl.pallas_call(
        functools.partial(layer_kernel, (peers, zs, rows, cols, ch)),
        out_shape=jax.ShapeDtypeStruct(frames.shape, BF16),
        in_specs=[in_hbm] * 6,
        out_specs=vmem,
        scratch_shapes=[
            pltpu.VMEM((count * rows + count, 32, ch), F32),
            pltpu.VMEM((count, rows + 2, cols, 3 * ch), BF16),
            pltpu.VMEM((count, rows + 2, cols, 3 * ch), BF16),
            pltpu.VMEM((n, count, step, cols, ch), F32),
            pltpu.VMEM((3, 3 * ch, ch), BF16),
            pltpu.VMEM((3, 3 * ch, ch), BF16),
            pieces, pieces, pieces, pieces,
            pltpu.VMEM((n, cols, lanes), F32),
            pltpu.VMEM((1, ch), jnp.int32),
            pltpu.VMEM((1, ch), F32),
            pltpu.VMEM((1, ch), F32),
            pltpu.VMEM((split, 1, lanes), F32),
            pltpu.VMEM((2, 2, count, rows // 2, ch), BF16),
            pltpu.VMEM((2, 2, count, rows // 2, ch), BF16),
            pltpu.VMEM((n, 2, count, step, ch), BF16),
            pltpu.VMEM((n, 2, count, step, ch), BF16),
            pltpu.VMEM((2, 2, count, ch), BF16),
            pltpu.VMEM((2, 2, count, ch), BF16),
            pltpu.VMEM((count * rows, cols, ch), F32),
            pltpu.VMEM((2, count, rows + 16, ch), F32),
            pltpu.VMEM((rows, cols, ch), F32),
            dma, dma((2,)), dma((3,)), dma((3,)), dma((n,)), dma, pltpu.SemaphoreType.REGULAR,
            dma((n + 2, 2)), dma((n + 2, 2)), dma((2,)), dma((2,)), dma((2, 2)), dma((2, 2)),
            dma((n,)), dma((n,)), dma((n,)), dma((n,)),
        ],
        compiler_params=pltpu.CompilerParams(
            collective_id=0, has_side_effects=True, vmem_limit_bytes=44 << 20
        ),
        name="layer",
    )(
        *(
            pltpu.with_memory_space_constraint(array, pltpu.HBM)
            for array in (
                frames,
                input_weight.reshape(3, 3 * ch, ch),
                output_weight.reshape(3, 3 * ch, ch),
                pole_index.reshape(1, ch),
                gelu_scale.reshape(1, ch),
                start_state,
            )
        )
    )


def solution(mesh):
    return jax.shard_map(
        functools.partial(on_device, mesh.shape["tm"], mesh.shape["sy"]),
        mesh=mesh,
        in_specs=(P("tm", "sx", "sy", None), P(), P(), P(), P(), P("sx", "sy", None)),
        out_specs=P("tm", "sx", "sy", None),
        check_vma=False,
    )
```

```python
import functools
import math

import jax
import jax.numpy as jnp
from jax import lax
from jax.experimental import pallas as pl
from jax.experimental.pallas import tpu as pltpu
from jax.sharding import PartitionSpec as P

NPOLES = 16
CHUNKS = 4
MESH = pl.DeviceIdType.MESH
F32 = jnp.float32
BF16 = jnp.bfloat16


def layer_kernel(
    sizes,
    frames_hbm, w1_hbm, w2_hbm, pole_hbm, scale_hbm, start_hbm, out,
    wide, xf, xm, drive, w1, w2, ends, gathered, prefixes, carried, first, pole_ref, scale_ref,
    decay_ref, decay2_ref, edge_out, edge_in, side_out, side_in, corner_out, corner_in, acc, beyond, tile,
    frame_sem, small_sem, w1_sem, w2_sem, first_sem, tile_sem, near_sem,
    col_send, col_recv, row_send, row_recv, corner_send, corner_recv,
    end_send, end_recv, pre_send, pre_recv,
):
    peers, zs, rows, cols, ch = sizes
    side = math.isqrt(peers)
    n = CHUNKS
    step = rows // n
    split = peers // step
    lanes = ch // split
    me, sx, z = lax.axis_index("tm"), lax.axis_index("sx"), lax.axis_index("sy")
    other = 1 - sx
    right, left = lax.rem(z + 1, zs), lax.rem(z + zs - 1, zs)
    has_left, has_right = z > 0, z < zs - 1
    goes, comes = (has_right, has_left), (has_left, has_right)

    def only(condition, action):
        def run():
            pl.when(condition)(lambda: action() and None)
        return run

    piece_row, piece_part = me // split, lax.rem(me, split)

    def row_of(lo, hi):
        return jnp.where(sx == 0, lo, rows - hi)

    def base(c):
        return row_of(c * step, (c + 1) * step)

    border = jnp.where(sx == 0, rows, 1)
    blank = jnp.where(sx == 0, 0, rows + 1)
    halo_there = blank
    halo_here = rows + 1 - blank

    y, x = me // side, lax.rem(me, side)
    in_row = [{"tm": y * side + lax.rem(x + k, side)} for k in range(1, side)]
    in_column = [{"tm": lax.rem(y + k, side) * side + x} for k in range(1, side)]
    around = in_row + in_column
    diagonal = [{"sx": other, "sy": right}, {"sx": other, "sy": left}]
    barrier = pltpu.get_barrier_semaphore()
    for where in [{"sx": other}] + around:
        pl.semaphore_signal(barrier, inc=1, device_id=where, device_id_type=MESH)
    for condition, to, corner in ((has_right, right, diagonal[0]), (has_left, left, diagonal[1])):
        @pl.when(condition)
        def _(to=to, corner=corner):
            for where in ({"sy": to}, corner):
                pl.semaphore_signal(barrier, inc=1, device_id=where, device_id_type=MESH)
    expected = 1 + len(around) + 2 * jnp.where(has_left, 1, 0) + 2 * jnp.where(has_right, 1, 0)

    mid = pl.ds(ch, ch)
    quarter = rows // 4
    for f in range(2):
        for part in range(4):
            pltpu.make_async_copy(
                frames_hbm.at[f, pl.ds(part * quarter, quarter)],
                xf.at[f, pl.ds(1 + part * quarter, quarter), :, mid], frame_sem,
            ).start()

    class Weight:
        def __init__(self, src, dst, sem, j):
            self.copies = [
                pltpu.make_async_copy(src.at[i, pl.ds(j * ch, ch)], dst.at[i, pl.ds(j * ch, ch)], sem)
                for i in range(3)
            ]
            self.whole = pltpu.make_async_copy(src.at[:, pl.ds(j * ch, ch)], dst.at[:, pl.ds(j * ch, ch)], sem)

        def start(self):
            for copy in self.copies:
                copy.start()

        def wait(self):
            self.whole.wait()

    def weight_copies(src, dst, sems):
        return [Weight(src, dst, sems.at[j], j) for j in range(3)]

    small_copies = [
        pltpu.make_async_copy(pole_hbm, pole_ref, small_sem.at[0]),
        pltpu.make_async_copy(scale_hbm, scale_ref, small_sem.at[1]),
    ]
    for copy in small_copies:
        copy.start()
    w1_copies = weight_copies(w1_hbm, w1, w1_sem)
    w1_copies[1].start()

    def tell():
        for where in in_row:
            pl.semaphore_signal(near_sem, inc=1, device_id=where, device_id_type=MESH)

    def hear():
        pl.semaphore_wait(near_sem, len(in_row))

    first_copies = []
    for c in range(n):
        copy = pltpu.make_async_copy(
            start_hbm.at[base(c) + piece_row, :, pl.ds(pl.multiple_of(piece_part * lanes, lanes), lanes)],
            first.at[c], first_sem.at[c],
        )
        copy.start()
        first_copies.append(copy)
    w2_copies = weight_copies(w2_hbm, w2, w2_sem)

    for d in range(2):
        @pl.when(jnp.logical_not(comes[d]))
        def _(d=d):
            edge_in[:, d] = jnp.zeros_like(edge_in[:, d])
            side_in[:, d] = jnp.zeros_like(side_in[:, d])
            corner_in[:, d] = jnp.zeros_like(corner_in[:, d])
    for padded in (xf, xm):
        padded[:, pl.ds(blank, 1)] = jnp.zeros((2, 1, cols, 3 * ch), BF16)

    def side_refs(slot):
        return (edge_out.at[slot - n], edge_in.at[slot - n]) if slot >= n else (side_out.at[slot], side_in.at[slot])

    def side_copies(slot):
        src, dst = side_refs(slot)
        return [
            pltpu.make_async_remote_copy(
                src.at[d], dst.at[d], col_send.at[slot, d], col_recv.at[slot, d],
                device_id={"sy": to}, device_id_type=MESH,
            )
            for d, to in ((0, right), (1, left))
        ]

    def row_copy(padded, slot):
        return pltpu.make_async_remote_copy(
            padded.at[:, pl.ds(border, 1), :, mid], padded.at[:, pl.ds(halo_there, 1), :, mid],
            row_send.at[slot], row_recv.at[slot],
            device_id={"sx": other}, device_id_type=MESH,
        )

    def border_copies(padded, slot):
        return [row_copy(padded, slot)] + [
            pltpu.make_async_remote_copy(
                corner_out.at[slot, d], corner_in.at[slot, d], corner_send.at[slot, d], corner_recv.at[slot, d],
                device_id=to, device_id_type=MESH,
            )
            for d, to in enumerate(diagonal)
        ]

    def start_border(copies):
        copies[0].start()
        for d, copy in enumerate(copies[1:]):
            only(goes[d], copy.start)()

    def fill_corners(slot):
        for d, col in ((0, 7 + cols), (1, 8)):
            corner_out[slot, d] = jnp.concatenate(
                [wide[f * rows + border - 1, col : col + 1, :] for f in range(2)], axis=0
            ).astype(BF16)

    def place_border(padded, slot, copies):
        sent.append(copies[0].wait_send)
        if slot == 0:
            copies[0].wait_recv()
        take(copies[1:])
        for f in range(2):
            at = 2 * rows + f
            wide[at, 8 : 8 + cols, :] = padded[f, halo_here, :, ch : 2 * ch].astype(F32)
            for d, col in ((0, 7), (1, 8 + cols)):
                wide[at, col : col + 1, :] = corner_in[slot, d].astype(F32)[f : f + 1]
            for j in (0, 2):
                padded[f, halo_here, :, j * ch : (j + 1) * ch] = wide[at, 7 + j : 7 + j + cols, :].astype(BF16)

    sent = []

    def flush(kept=0):
        while len(sent) > kept:
            sent.pop(0)()

    def send_sides(slot, at, count):
        src = side_refs(slot)[0]
        for f in range(2):
            spot = pl.ds(f * rows + at, count)
            last, head = wide[spot, 7 + cols, :], wide[spot, 8, :]
            src[0, f] = last.astype(BF16)
            src[1, f] = head.astype(BF16)
        if slot == n:
            fill_corners(0)
            pl.semaphore_wait(barrier, expected)
            tell()
        copies = side_copies(slot)
        for d, copy in enumerate(copies):
            only(goes[d], copy.start)()
        return copies

    def take(copies):
        for d, copy in enumerate(copies):
            only(comes[d], copy.wait_recv)()
            sent.append(only(goes[d], copy.wait_send))

    def place_sides(slot, at, count):
        dst = side_refs(slot)[1]
        for f in range(2):
            spot = pl.ds(f * rows + at, count)
            for d, col in ((0, 7), (1, 8 + cols)):
                wide[spot, col, :] = dst[d, f].astype(F32)

    def spread(padded, at, count):
        for f in range(2):
            for r in range(count):
                for j in (0, 2):
                    padded[f, at + r + 1, :, j * ch : (j + 1) * ch] = wide[f * rows + at + r, 7 + j : 7 + j + cols, :].astype(BF16)

    def dots(padded, weight, at, count, js):
        left_side = jnp.concatenate(
            [
                padded[:, pl.ds(at + i, count), :, j * ch : (j + 1) * ch].reshape(2 * count * cols, ch)
                for i in range(3) for j in js
            ],
            axis=-1,
        )
        right_side = jnp.concatenate([weight[i, j * ch : (j + 1) * ch] for i in range(3) for j in js], axis=0)
        return jnp.dot(left_side, right_side, preferred_element_type=F32).reshape(2, count, cols, ch)

    pltpu.make_async_copy(frames_hbm, xf.at[:, pl.ds(1, rows), :, mid], frame_sem).wait()
    w1_copies[0].start()
    w1_copies[2].start()

    def widen(r, _):
        for f in range(2):
            wide[f * rows + r, 8 : 8 + cols, :] = xf[f, r + 1, :, ch : 2 * ch].astype(F32)
        return 0

    lax.fori_loop(0, rows, widen, 0, unroll=4)
    half = rows // 2
    early = send_sides(n, row_of(0, half), half)
    late = send_sides(n + 1, row_of(half, rows), half)
    border_f = border_copies(xf, 0)
    start_border(border_f)
    for copy in small_copies:
        copy.wait()
    decay = jnp.exp(-0.001 * jnp.exp(pole_ref[...].astype(F32) * (math.log(300.0) / (NPOLES - 1))))
    decay_ref[...] = decay
    for part in range(split):
        decay2_ref[part] = (decay * decay)[:, part * lanes : (part + 1) * lanes]
    w1_copies[1].wait()
    for c in range(n - 1):
        drive[c] = dots(xf, w1, base(c), step, (1,))
    take(early)
    for copy in w2_copies:
        copy.start()
    tile_copy = pltpu.make_async_copy(start_hbm, tile, tile_sem)
    only(me == 0, tile_copy.start)()
    place_sides(n, row_of(0, half), half)
    spread(xf, row_of(0, step + 1), step + 1)
    w1_copies[0].wait()
    w1_copies[2].wait()

    def all_of(ref, sem):
        return pltpu.make_async_copy(ref, ref, sem)

    def transfer(src, dst, send, recv, c, to):
        return pltpu.make_async_remote_copy(
            src.at[c, to], dst.at[c, me], send.at[c], recv.at[c], device_id={"tm": to}, device_id_type=MESH
        )

    is_last, is_first = me == peers - 1, me == 0

    def send_ends(c):
        @pl.when(jnp.logical_not(is_last))
        def _():
            pltpu.make_async_copy(ends.at[c, me], gathered.at[c, me], end_recv.at[c]).start()
            for k in range(1, peers):
                transfer(ends, gathered, end_send, end_recv, c, lax.rem(me + k, peers)).start()

        sent.append(only(jnp.logical_not(is_last), all_of(ends.at[c, pl.ds(0, peers - 1)], end_send.at[c]).wait))

    def send_prefixes(c):
        @pl.when(jnp.logical_not(is_first))
        def _():
            pltpu.make_async_copy(prefixes.at[c, me], carried.at[c, me], pre_recv.at[c]).start()

        for k in range(1, peers):
            to = lax.rem(me + k, peers)
            only(to != 0, transfer(prefixes, carried, pre_send, pre_recv, c, to).start)()

        def settle():
            only(is_first, all_of(prefixes.at[c, pl.ds(0, peers - 1)], pre_send.at[c]).wait)()
            only(jnp.logical_not(is_first), all_of(prefixes.at[c, pl.ds(0, peers - 2)], pre_send.at[c]).wait)()

        sent.append(settle)

    def drive_chunk(c):
        if c < n - 1:
            got = drive[c] + dots(xf, w1, base(c), step, (0, 2))
        else:
            got = dots(xf, w1, base(c), step, (0, 1, 2))
        drive[c] = got
        end = decay_ref[...].reshape(1, 1, ch) * got[0] + got[1]
        for r in range(step):
            for part in range(split):
                ends[c, r * split + part] = end[r, :, part * lanes : (part + 1) * lanes].astype(BF16)
        if c == 0:
            hear()
        send_ends(c)

    def prefix_chunk(c):
        first_copies[c].wait()
        all_of(gathered.at[c, pl.ds(0, peers - 1)], end_recv.at[c]).wait()
        square = decay2_ref[pl.ds(piece_part, 1)].reshape(1, lanes)
        state = first[c]
        for i in range(peers):
            prefixes[c, i] = state.astype(BF16)
            if i < peers - 1:
                state = square * state + gathered[c, i].astype(F32)
        send_prefixes(c)

    def mix_chunk(c):
        if c == 0:
            flush(n)
        only(jnp.logical_not(is_first), all_of(carried.at[c], pre_recv.at[c]).wait)()
        at = base(c)
        for r in range(step):
            state = jnp.concatenate([carried[c, r * split + part] for part in range(split)], axis=-1).astype(F32)
            for f in range(2):
                state = decay_ref[...] * state + drive[c, f, r]
                mixed = jax.nn.gelu(scale_ref[...] * state)
                wide[f * rows + at + r, 8 : 8 + cols, :] = mixed
                xm[f, at + r + 1, :, ch : 2 * ch] = mixed.astype(BF16)
        if c == n - 1:
            fill_corners(1)
            start_border(border_m)
        sides[c] = send_sides(c, at, step)
        spread(xm, at, step)

    sides = {}
    border_m = border_copies(xm, 1)

    def window(c):
        lo = max(c * step - 1, 0)
        hi = rows if c == n - 1 else (c + 1) * step - 1
        return row_of(lo, hi), hi - lo

    def gather_chunk(c, js, more=False):
        at, count = window(c)
        got = dots(xm, w2, at, count, js)
        for f in range(2):
            spot = pl.ds(f * rows + at, count)
            acc[spot] = acc[spot] + got[f] if more else got[f]

    def border_row():
        border_m[0].wait_recv()
        sent.append(border_m[0].wait_send)
        for f in range(2):
            at = 2 * rows + f
            wide[at, 8 : 8 + cols, :] = xm[f, halo_here, :, ch : 2 * ch].astype(F32)
            for j in (0, 2):
                xm[f, halo_here, :, j * ch : (j + 1) * ch] = wide[at, 7 + j : 7 + j + cols, :].astype(BF16)

    def clear_sides():
        none = jnp.zeros((2 * rows + 2, ch), F32)
        for col in (7, 8 + cols):
            wide[:, col, :] = none

    def beyond_chunk(c):
        take(sides[c])
        at = pl.multiple_of(base(c) + 8, 8)
        for d in range(2):
            for f in range(2):
                beyond[d, f, pl.ds(at, step), :] = side_in[c, d, f].astype(F32)

    def beyond_corners():
        take(border_m[1:])
        for d in range(2):
            corner = corner_in[1, d].astype(F32)
            for f in range(2):
                row = corner[f : f + 1]
                beyond[d, f, 7:8, :] = jnp.where(sx == 1, row, 0.0)
                beyond[d, f, 8 + rows : 9 + rows, :] = jnp.where(sx == 0, row, 0.0)

    def finish(at, count):
        for d, j, col in ((0, 0, 0), (1, 2, cols - 1)):
            parts = []
            for f in range(2):
                view = beyond.at[d, f, pl.ds(pl.multiple_of(at, 8), count + 16), :]
                parts.append(
                    jnp.concatenate([view[7 + i : 7 + i + count, :].astype(BF16) for i in range(3)], axis=-1)
                )
            left_side = jnp.concatenate(parts, axis=0)
            right_side = jnp.concatenate([w2[i, j * ch : (j + 1) * ch] for i in range(3)], axis=0)
            got = jnp.dot(left_side, right_side, preferred_element_type=F32)
            for f in range(2):
                spot = pl.ds(f * rows + at, count)
                acc[spot, col, :] = acc[spot, col, :] + got[f * count : (f + 1) * count]

        def narrow(r, _):
            for f in range(2):
                out[f, at + r] = acc[f * rows + at + r].astype(BF16)
            return 0

        lax.fori_loop(0, count, narrow, 0, unroll=8)

    drive_chunk(0)
    take(late)
    place_sides(n + 1, row_of(half, rows), half)
    spread(xf, row_of(step + 1, 2 * step + 1), step)
    drive_chunk(1)
    spread(xf, row_of(2 * step + 1, rows), rows - 2 * step - 1)
    drive_chunk(2)
    place_border(xf, 0, border_f)
    drive_chunk(3)
    clear_sides()

    @pl.when(is_first)
    def _():
        tile_copy.wait()
        for c in range(n):
            for r in range(step):
                for part in range(split):
                    carried[c, r * split + part] = tile[
                        base(c) + r, :, part * lanes : (part + 1) * lanes
                    ].astype(BF16)

    for c in range(n):
        prefix_chunk(c)
    for copy in w2_copies:
        copy.wait()
    every = (0, 1, 2)
    mix_chunk(0)
    gather_chunk(0, every)
    mix_chunk(1)
    gather_chunk(1, (1,))
    mix_chunk(2)
    gather_chunk(2, (1,))
    mix_chunk(3)
    gather_chunk(1, (0, 2), True)
    gather_chunk(2, (0, 2), True)
    border_row()
    gather_chunk(3, every)
    flush()
    beyond[:, :, 7:8, :] = jnp.zeros((2, 2, 1, ch), F32)
    beyond[:, :, 8 + rows : 9 + rows, :] = jnp.zeros((2, 2, 1, ch), F32)
    for c in range(n - 1):
        beyond_chunk(c)
    finish(row_of(0, half), half)
    beyond_chunk(n - 1)
    beyond_corners()
    finish(row_of(half, rows), half)
    flush()


def on_device(peers, zs, frames, input_weight, output_weight, pole_index, gelu_scale, start_state):
    count, rows, cols, ch = frames.shape
    n = CHUNKS
    step = rows // n
    split = peers // step
    lanes = ch // split
    in_hbm = pl.BlockSpec(memory_space=pltpu.HBM)
    vmem = pl.BlockSpec(memory_space=pltpu.VMEM)
    dma = pltpu.SemaphoreType.DMA
    pieces = pltpu.VMEM((n, peers, cols, lanes), BF16)
    return pl.pallas_call(
        functools.partial(layer_kernel, (peers, zs, rows, cols, ch)),
        out_shape=jax.ShapeDtypeStruct(frames.shape, BF16),
        in_specs=[in_hbm] * 6,
        out_specs=vmem,
        scratch_shapes=[
            pltpu.VMEM((count * rows + count, 32, ch), F32),
            pltpu.VMEM((count, rows + 2, cols, 3 * ch), BF16),
            pltpu.VMEM((count, rows + 2, cols, 3 * ch), BF16),
            pltpu.VMEM((n, count, step, cols, ch), F32),
            pltpu.VMEM((3, 3 * ch, ch), BF16),
            pltpu.VMEM((3, 3 * ch, ch), BF16),
            pieces, pieces, pieces, pieces,
            pltpu.VMEM((n, cols, lanes), F32),
            pltpu.VMEM((1, ch), jnp.int32),
            pltpu.VMEM((1, ch), F32),
            pltpu.VMEM((1, ch), F32),
            pltpu.VMEM((split, 1, lanes), F32),
            pltpu.VMEM((2, 2, count, rows // 2, ch), BF16),
            pltpu.VMEM((2, 2, count, rows // 2, ch), BF16),
            pltpu.VMEM((n, 2, count, step, ch), BF16),
            pltpu.VMEM((n, 2, count, step, ch), BF16),
            pltpu.VMEM((2, 2, count, ch), BF16),
            pltpu.VMEM((2, 2, count, ch), BF16),
            pltpu.VMEM((count * rows, cols, ch), F32),
            pltpu.VMEM((2, count, rows + 16, ch), F32),
            pltpu.VMEM((rows, cols, ch), F32),
            dma, dma((2,)), dma((3,)), dma((3,)), dma((n,)), dma, pltpu.SemaphoreType.REGULAR,
            dma((n + 2, 2)), dma((n + 2, 2)), dma((2,)), dma((2,)), dma((2, 2)), dma((2, 2)),
            dma((n,)), dma((n,)), dma((n,)), dma((n,)),
        ],
        compiler_params=pltpu.CompilerParams(
            collective_id=0, has_side_effects=True, vmem_limit_bytes=44 << 20
        ),
        name="layer",
    )(
        *(
            pltpu.with_memory_space_constraint(array, pltpu.HBM)
            for array in (
                frames,
                input_weight.reshape(3, 3 * ch, ch),
                output_weight.reshape(3, 3 * ch, ch),
                pole_index.reshape(1, ch),
                gelu_scale.reshape(1, ch),
                start_state,
            )
        )
    )


def solution(mesh):
    return jax.shard_map(
        functools.partial(on_device, mesh.shape["tm"], mesh.shape["sy"]),
        mesh=mesh,
        in_specs=(P("tm", "sx", "sy", None), P(), P(), P(), P(), P("sx", "sy", None)),
        out_specs=P("tm", "sx", "sy", None),
        check_vma=False,
    )
```
